32 devices in a mesh: group: 2 (over x), ep: 4 (over y, core), kv: 4 (over z).
Axes of the slice: x: 2, y: 2, z: 4, core: 2. Of those that a mesh axis runs over, the one named last changes fastest.
Arguments:
- queries: bfloat16 [1024, 4096], P(('group', 'ep', 'kv')), parts along dimension 0, may hold values from -8 to 8
- new_keys: bfloat16 [1024, 512], P(('group', 'ep', 'kv')), parts along dimension 0, may hold values from -6 to 6
- new_values: bfloat16 [1024, 512], P(('group', 'ep', 'kv')), parts along dimension 0, may hold values from -6 to 6
- key_cache: bfloat16 [8, 16384, 512], P(('group', 'ep'), 'kv'), parts along dimension 0, may hold values from -8 to 8
- value_cache: bfloat16 [8, 16384, 512], P(('group', 'ep'), 'kv'), parts along dimension 0, may hold values from -6 to 6
- lengths: int32 [8], P(('group', 'ep')), parts along dimension 0, may hold values from 2 to 16384, as said below
- residual_in: bfloat16 [1024, 2048], P(('group', 'ep', 'kv')), parts along dimension 0, may hold values from -20 to 20
- out_weight: bfloat16 [4096, 2048], P('kv'), may hold values from -0.25 to 0.25
- norm_gain: float32 [2048], replicated, may hold values from 0.5 to 1.5
- gate_up_weight: bfloat16 [16, 2048, 1536], P(('ep', 'kv')), may hold values from -0.125 to 0.125
- down_weight: bfloat16 [16, 768, 2048], P(('ep', 'kv')), may hold values from -0.21875 to 0.21875
- expert_ids: int32 [1024, 8], P(('group', 'ep', 'kv')), parts along dimension 0, may hold values from 0 to 15, all different within a row; in each aligned block of 32 rows (0 to 31, 32 to 63, ...) at most 32 rows name the same one
- route_weights: float32 [1024, 8], P(('group', 'ep', 'kv')), parts along dimension 0, may hold values from 0.05 to 1
Outputs:
- layer_out: bfloat16 [1024, 2048], P(('group', 'ep', 'kv')), parts along dimension 0
The draws below stay inside these ranges and needn't reach their ends.
There are 2 independent parts, one for each index of `group`. The reference program is written for one: setup_inputs(seed, part) draws one part's arguments, and reference() takes and returns one part's arrays. A program takes and returns all parts, laid end to end along the dimension named above; an argument that names none is the same for every part. Nothing has to cross between parts.
Inputs may be any that keep to these rules, and one draw needn't show every extreme that they name: `lengths`: some request of each group has all 16384 positions filled. `expert_ids`: each row names 8 different experts; within the rows of one device (aligned blocks of 32 rows) no expert is named more than 32 times, a bound that some block reaches.
All inputs are finite; a program needn't handle non-finite values.
Results may differ from the reference program's by a relative error of at most 0.019.
Values may be sent and summed in bfloat16 or wider, within the bound.
No kernel may reach another device: no remote copies, remote signals or barrier semaphores. Data moves between devices by JAX's collectives and lax.ppermute only.
A program may use at most 192 MiB of HBM per device.

```python
import math
import jax
import jax.numpy as jnp
import numpy as np
from jax import lax

D = 2048
QH = 32
KVH = 4
HD = 128
FF = 768
TOPK = 8
BLOCK = 128
CTX = 16384
REQ = 4
ROWS = 512
ROWS_DEV = 32
EXPERTS = 16
CAP = 32
N_EP = 4
N_KV = 4


def shared_direction(key):
    return (2 * jax.random.randint(jax.random.fold_in(key, 101), (HD,), 0, 2) - 1).astype(jnp.float32)


def draw_queries(key, part):
    noise_key = jax.random.fold_in(key, 1)
    sample = jnp.clip(2.0 * jax.random.normal(noise_key, (ROWS, QH * HD), jnp.float32), -8.0, 8.0)
    aligned = jnp.tile(shared_direction(key), QH)
    position = jnp.arange(ROWS) % BLOCK
    sample = jnp.where((position == 5)[:, None], 8.0 * aligned[None, :], sample)
    sample = jnp.where((position == 9)[:, None], 4.0 * aligned[None, :], sample)
    return sample.astype(jnp.bfloat16)


def draw_key_cache(key, part):
    noise_key = jax.random.fold_in(key, 2)
    sample = jnp.clip(jax.random.normal(noise_key, (REQ, CTX, KVH * HD), jnp.float32), -6.0, 6.0)
    aligned = jnp.tile(shared_direction(key), KVH)
    second = 8.0 - 0.25 / jnp.sqrt(float(HD))
    sample = sample.at[:, 0, :].set(8.0 * aligned)
    sample = sample.at[:, 1, :].set(second * aligned)
    return sample.astype(jnp.bfloat16)


def draw_residual_in(key, part):
    row_scale = jnp.exp(jax.random.uniform(jax.random.fold_in(key, 4), (ROWS, 1), jnp.float32, 0.0, jnp.log(10.0)))
    column_scale = jnp.exp(jax.random.uniform(jax.random.fold_in(key, 5), (1, D), jnp.float32, 0.0, jnp.log(10.0)))
    sample = jnp.clip(jax.random.normal(jax.random.fold_in(key, 3), (ROWS, D), jnp.float32), -4.0, 4.0)
    return (0.05 * sample * row_scale * column_scale).astype(jnp.bfloat16)


def draw_lengths(key, part):
    drawn = jax.random.randint(jax.random.fold_in(key, 7), (REQ,), 2, CTX + 1).astype(jnp.int32)
    return drawn.at[0].set(CTX)


def shard_levels(own_key, shape, split, least, largest):
    loudness = 1.0
    for dim, shards_of in split:
        heights = jax.random.uniform(jax.random.fold_in(jax.random.fold_in(own_key, 6), dim), (shards_of,), jnp.float32, least / len(split), largest / len(split))
        loudness = loudness * jnp.repeat(jnp.exp(heights), shape[dim] // shards_of).reshape((-1,) + (1,) * (len(shape) - 1 - dim))
    return loudness


def assign_block(stream_key, own, number, rows, count, top, bound, skew):
    order = jax.random.permutation(stream_key, count)
    crowded, usual = load_shares(count, rows * top, bound, skew, True), load_shares(count, rows * top, bound, skew, False)
    places = jnp.arange(count)

    def named(sizes, rotation):
        used = int((sizes > 0).sum())
        fixed = max(1, used // 4)
        passed = fixed + (places - fixed + rotation * (used - fixed)) % max(1, count - fixed)
        return jnp.zeros((count,), jnp.int32).at[order[jnp.where(places < fixed, places, passed)]].set(jnp.asarray(sizes, jnp.int32))

    sizes = jnp.where(number % 4 == 0, named(crowded, number // 4), named(usual, number - number // 4 - 1))
    mixed = jax.random.permutation(jax.random.fold_in(own, 3), count)
    giver, receiver = mixed[0:count // 2 * 2:2], mixed[1:count // 2 * 2:2]
    slack = jnp.minimum(sizes[giver] - 1, bound - sizes[receiver]) // 2
    slack = jnp.where((giver == order[0]) | (receiver == order[0]) | (sizes[receiver] == 0), 0, jnp.maximum(slack, 0))
    passed = jax.random.randint(jax.random.fold_in(own, 4), (count // 2,), 0, 1 << 20) % (slack + 1)
    sizes = sizes.at[giver].add(-passed).at[receiver].add(passed)
    items = jnp.searchsorted(jnp.cumsum(sizes), jnp.arange(rows * top), side="right").astype(jnp.int32)
    listing = items.reshape(top, rows).T
    listing = listing[jax.random.permutation(jax.random.fold_in(own, 1), rows)]
    rotation = jax.random.randint(jax.random.fold_in(own, 2), (rows, 1), 0, top)
    return jnp.take_along_axis(listing, (jnp.arange(top)[None, :] + rotation) % top, axis=1)


def load_shares(amount, total, reach, slope, full):
    weights = [(1 << 20) // math.isqrt(standing ** slope) + 1 for standing in range(1, amount + 1)]
    largest = reach if full else min(reach, max(-(-total // amount), total * weights[0] // sum(weights)))
    least = 1 if total - largest >= amount - 1 else 0
    holding, spare = [largest] + [least] * (amount - 1), total - largest - least * (amount - 1)
    while spare > 0:
        candidates = [i for i in range(1, amount) if holding[i] < largest] or [i for i in range(1, amount) if holding[i] < reach]
        whole, left = sum([weights[i] for i in candidates]), spare
        for i in candidates:
            addition = min(reach - holding[i], max(1, left * weights[i] // whole), spare)
            holding[i] = holding[i] + addition
            spare = spare - addition
    return np.array(holding)


def noise(rng, shape, spread, most, pieces=(), held_as=jnp.bfloat16):
    level = shard_levels(rng, shape, pieces, -0.22, 0.18) if pieces else 1.0
    entries = jax.random.normal(rng, shape, jnp.float32) * spread * level
    return jnp.minimum(jnp.maximum(entries, -most), most).astype(held_as)


def setup_inputs(seed: int = 0, part: int = 0) -> dict:
    key_of = jax.random.split(jax.random.key(seed), 14)
    part_keys = jax.random.split(jax.random.fold_in(key_of[13], part), 14)
    queries = draw_queries(jax.random.fold_in(jax.random.fold_in(key_of[13], part), 71), part)
    new_keys = noise(part_keys[1], (ROWS, KVH * HD), 1.0, 6.0, ((0, 16),))
    new_values = noise(part_keys[2], (ROWS, KVH * HD), 1.0, 6.0, ((0, 16),))
    key_cache = draw_key_cache(jax.random.fold_in(jax.random.fold_in(key_of[13], part), 71), part)
    value_cache = noise(part_keys[4], (REQ, CTX, KVH * HD), 1.0, 6.0, ((0, 4), (1, 4)))
    lengths = draw_lengths(jax.random.fold_in(jax.random.fold_in(key_of[13], part), 71), part)
    residual_in = draw_residual_in(jax.random.fold_in(jax.random.fold_in(key_of[13], part), 71), part)
    out_weight = noise(key_of[7], (QH * HD, D), (HD * KVH) ** -0.5, 0.25, ((0, 4),))
    norm_gain = jnp.clip(1.0 + 0.1 * jax.random.normal(key_of[8], (D,), jnp.float32), 0.5, 1.5)
    gate_up_weight = noise(key_of[9], (EXPERTS, D, 2 * FF), D ** -0.5, 0.125, ((0, 16),))
    down_weight = noise(key_of[10], (EXPERTS, FF, D), FF ** -0.5, 0.21875, ((0, 16),))
    expert_ids_keys = jax.random.split(jax.random.fold_in(part_keys[11], 1), ROWS // ROWS_DEV)
    expert_ids_turns = jax.random.permutation(jax.random.fold_in(part_keys[11], 3), ROWS // ROWS_DEV)
    expert_ids = jax.vmap(lambda own, number: assign_block(jax.random.fold_in(part_keys[11], 2), own, number, ROWS_DEV, EXPERTS, TOPK, CAP, 2))(expert_ids_keys, expert_ids_turns).reshape((ROWS, TOPK))
    route_weights = jnp.clip(jnp.exp(math.log(1.0) - 2.9957323 * jax.random.uniform(part_keys[12], (ROWS, TOPK), jnp.float32) ** shard_levels(part_keys[12], (ROWS, TOPK), ((0, 16),), -0.2, 0.2)), 0.05, 1.0)
    return {"queries": queries, "new_keys": new_keys, "new_values": new_values, "key_cache": key_cache, "value_cache": value_cache, "lengths": lengths, "residual_in": residual_in, "out_weight": out_weight, "norm_gain": norm_gain, "gate_up_weight": gate_up_weight, "down_weight": down_weight, "expert_ids": expert_ids, "route_weights": route_weights}


masked_score = -1e+30
norm_epsilon = 1e-06

def attend_request(inputs):
    query_rows, cache_keys, cache_values, fresh_keys, fresh_values, length = inputs
    group_size = QH // KVH
    key_rows = jnp.concatenate([cache_keys, fresh_keys], axis=0).astype(jnp.float32).reshape(CTX + BLOCK, KVH, HD)
    value_rows = jnp.concatenate([cache_values, fresh_values], axis=0).astype(jnp.float32).reshape(CTX + BLOCK, KVH, HD)
    query_grid = query_rows.astype(jnp.float32).reshape(BLOCK, KVH, group_size, HD)
    scores = jnp.einsum('cgqd,pgd->gqcp', query_grid, key_rows) * HD ** (-0.5)
    position = jnp.arange(CTX + BLOCK, dtype=jnp.int32)
    query_position = jnp.arange(BLOCK, dtype=jnp.int32)
    visible = jnp.where(position[None, :] < CTX, position[None, :] < length, position[None, :] - CTX <= query_position[:, None])
    scores = jnp.where(visible, scores, masked_score)
    row_max = lax.optimization_barrier(jnp.max(scores, axis=-1, keepdims=True))
    probs = jnp.where(visible, jnp.exp(scores - row_max), 0.0)
    row_sum = lax.optimization_barrier(jnp.sum(probs, axis=-1))
    rounded = lax.optimization_barrier(probs.astype(jnp.bfloat16)).astype(jnp.float32)
    numerator = jnp.einsum('gqcp,pgd->cgqd', rounded, value_rows)
    result = numerator / jnp.transpose(row_sum, (2, 0, 1))[..., None]
    return result.reshape(BLOCK, QH * HD).astype(jnp.bfloat16)

def reference(queries, new_keys, new_values, key_cache, value_cache, lengths, residual_in, out_weight, norm_gain, gate_up_weight, down_weight, expert_ids, route_weights):
    attention = lax.map(attend_request, (queries.reshape(REQ, BLOCK, QH * HD), key_cache, value_cache, new_keys.reshape(REQ, BLOCK, KVH * HD), new_values.reshape(REQ, BLOCK, KVH * HD), lengths))
    attention = attention.reshape(ROWS, QH * HD)
    projected = jnp.dot(attention, out_weight, preferred_element_type=jnp.float32)
    hidden_state = residual_in.astype(jnp.float32) + projected
    normed = (hidden_state * lax.rsqrt(lax.optimization_barrier(jnp.mean(hidden_state * hidden_state, axis=-1, keepdims=True)) + norm_epsilon) * norm_gain).astype(jnp.bfloat16)
    pair_count = ROWS * TOPK
    pair_expert = expert_ids.reshape(-1).astype(jnp.int32)
    pair_row = jnp.arange(pair_count, dtype=jnp.int32) // TOPK
    pair_gate = route_weights.reshape(-1)
    capacity_all = N_EP * N_KV * CAP

    def apply_expert(running, inputs):
        expert_index, up_matrix, down_matrix = inputs
        matches = pair_expert == expert_index
        picked = jnp.nonzero(matches, size=capacity_all, fill_value=pair_count)[0].astype(jnp.int32)
        filled = picked < pair_count
        clamped = jnp.minimum(picked, pair_count - 1)
        target_rows = pair_row[clamped]
        gathered = normed[target_rows]
        mixed = jnp.dot(gathered, up_matrix, preferred_element_type=jnp.float32)
        expert_hidden = (jax.nn.silu(mixed[:, :FF]) * mixed[:, FF:]).astype(jnp.bfloat16)
        expert_out = jnp.dot(expert_hidden, down_matrix, preferred_element_type=jnp.float32).astype(jnp.bfloat16)
        expert_out = lax.optimization_barrier(expert_out).astype(jnp.float32)
        weight = jnp.where(filled, pair_gate[clamped], 0.0)
        return (running.at[target_rows].add(weight[:, None] * expert_out), None)
    start_value = jnp.zeros((ROWS, D), jnp.float32)
    mixture, unused = lax.scan(apply_expert, start_value, (jnp.arange(EXPERTS, dtype=jnp.int32), gate_up_weight, down_weight))
    return (hidden_state + mixture).astype(jnp.bfloat16)
```

```python
import functools
import math

import jax
import jax.numpy as jnp
from jax import lax
from jax.experimental import pallas as pl
from jax.experimental.pallas import tpu as pltpu
from jax.sharding import PartitionSpec as P

D = 2048
QH = 32
KVH = 4
HD = 128
FF = 768
TOPK = 8
BLOCK = 128

absent = -1e30
masked_score = -3e38
norm_epsilon = 1e-06
score_scale = math.log2(math.e) * HD**-0.5
key_step = 512
f32 = jnp.float32
bf16 = jnp.bfloat16

VM = pl.BlockSpec(memory_space=pltpu.VMEM)
HBM = pl.BlockSpec(memory_space=pl.ANY)
SM = pl.BlockSpec(memory_space=pltpu.SMEM)


def shifted(array, axis, by):
    size = lax.axis_size(axis)
    if by % size == 0:
        return array
    return lax.ppermute(array, axis, [(i, (i + by) % size) for i in range(size)])


def swapped(array, axis, bit):
    return lax.ppermute(array, axis, [(i, i ^ bit) for i in range(lax.axis_size(axis))])


def scored(left, right):
    return lax.dot_general(left, right, (((1,), (1,)), ((), ())), preferred_element_type=f32)


def three_parts(value):
    first = value.astype(bf16).astype(f32)
    rest = value - first
    second = rest.astype(bf16).astype(f32)
    return first, second, rest - second


def attend(bounds, blocks, places, query_chunks, keys, values, fresh_keys, fresh_values, heads):
    count = len(query_chunks)
    rows = query_chunks[0].shape[0]
    block_count = QH // heads
    per_key_head = QH // KVH // heads
    cached = keys.shape[0]
    fresh = fresh_keys.shape[0]
    padded = cached + 128
    width = heads * HD
    size = count * heads * rows

    def body(*refs):
        bounds_ref, blocks_ref, places_ref = refs[:3]
        query_refs = refs[3 : 3 + count]
        key_hbm, value_hbm, fresh_key_ref, fresh_value_ref = refs[3 + count : 7 + count]
        outs = refs[7 + count : 7 + count + block_count]
        keys_in, values_in, ones, even, odd, largest, sems = refs[7 + count + block_count :]
        score_refs = (even, odd)
        filled = bounds_ref[0]
        fresh_start = bounds_ref[1]

        def lane_of(i):
            return pl.multiple_of((blocks_ref[i] // per_key_head) * HD, HD)

        def copies(i):
            lanes = pl.ds(lane_of(i), HD)
            return (
                pltpu.make_async_copy(key_hbm.at[:, lanes], keys_in.at[i, pl.ds(0, cached)], sems.at[0, i]),
                pltpu.make_async_copy(value_hbm.at[:, lanes], values_in.at[i, pl.ds(0, cached)], sems.at[1, i]),
            )

        for i in range(block_count):
            for copy in copies(i):
                copy.start()
        place = lax.broadcasted_iota(jnp.int32, (padded, HD), 0)
        counted = (place < filled) | ((place >= cached) & (place < cached + fresh))
        ones[...] = jnp.where(counted, 1.0, 0.0).astype(bf16)
        blank = jnp.zeros((128 - fresh, HD), bf16)
        for i in range(block_count):
            lanes = pl.ds(lane_of(i), HD)
            keys_in[i, cached : cached + fresh] = fresh_key_ref[:, lanes]
            keys_in[i, cached + fresh :] = blank
            values_in[i, cached : cached + fresh] = fresh_value_ref[:, lanes]
            values_in[i, cached + fresh :] = blank

        def arrive(i):
            for copy in copies(i):
                copy.wait()

            @pl.when(filled < cached)
            def _():
                inside = lax.broadcasted_iota(jnp.int32, (cached, HD), 0) < filled
                held = keys_in[i, :cached]
                keys_in[i, :cached] = jnp.where(inside, held, jnp.broadcast_to(held[:1], held.shape))
                values_in[i, :cached] = jnp.where(inside, values_in[i, :cached], jnp.zeros((cached, HD), bf16))

        def fill_scores(i):
            out = score_refs[i % 2]
            lanes = pl.ds(pl.multiple_of(blocks_ref[i] * width, HD), width)
            chunks = [ref[:, lanes].astype(f32) * score_scale for ref in query_refs]
            stacked = jnp.concatenate([c[:, h * HD : (h + 1) * HD] for c in chunks for h in range(heads)], 0)
            high = stacked.astype(bf16)
            both = jnp.concatenate([high, (stacked - high.astype(f32)).astype(bf16)], 1)
            running = None
            for start in range(0, cached, key_step):
                part = keys_in[i, start : start + key_step]
                scores = scored(both, jnp.concatenate([part, part], 1))
                out[:, start : start + key_step] = scores
                for at in range(0, key_step, HD):
                    piece = scores[:, at : at + HD]
                    running = piece if running is None else jnp.maximum(running, piece)
            part = keys_in[i, cached:]
            scores = scored(both, jnp.concatenate([part, part], 1))
            row = lax.broadcasted_iota(jnp.int32, (rows, HD), 0)
            column = lax.broadcasted_iota(jnp.int32, (rows, HD), 1)
            masked = []
            for c in range(count):
                seen = (column < fresh) & (column + fresh_start <= row + places_ref[c] * rows)
                own = scores[c * heads * rows : (c + 1) * heads * rows]
                masked.append(jnp.where(jnp.tile(seen, (heads, 1)), own, masked_score))
            scores = jnp.concatenate(masked, 0)
            out[:, cached:] = scores
            running = jnp.maximum(running, scores)
            top = jnp.maximum(jnp.max(running, 1, keepdims=True), absent)
            largest[i % 2] = jnp.broadcast_to(top, (size, HD))

        def weigh(i):
            slot = i % 2
            top = largest[slot]
            probs = jnp.exp2(score_refs[slot][...] - top[:, :1]).astype(bf16)
            both = jnp.concatenate([values_in[i], ones[...]], 1)
            total = jnp.dot(probs, both, preferred_element_type=f32)
            lane = lax.broadcasted_iota(jnp.int32, (rows, HD), 1)
            for c in range(count):
                stats = jnp.zeros((rows, HD), f32)
                for h in range(heads):
                    at = (c * heads + h) * rows
                    piece = total[at : at + rows]
                    norm = piece[:, HD:]
                    some = norm > 0
                    safe = jnp.where(some, norm, 1.0)
                    outs[i][c, :, h * HD : (h + 1) * HD] = (piece[:, :HD] / safe).astype(bf16)
                    level = jnp.where(some, top[at : at + rows] + jnp.log2(safe), absent)
                    for k, part in enumerate(three_parts(level)):
                        stats = jnp.where(lane == h + k * heads, part, stats)
                outs[i][c, :, width:] = stats.astype(bf16)

        arrive(0)
        fill_scores(0)
        for i in range(1, block_count):
            arrive(i)
            fill_scores(i)
            weigh(i - 1)
        weigh(block_count - 1)

    return pl.pallas_call(
        body,
        in_specs=[SM] * 3 + [VM] * count + [HBM] * 2 + [VM] * 2,
        out_specs=[VM] * block_count,
        out_shape=[jax.ShapeDtypeStruct((count, rows, width + HD), bf16)] * block_count,
        scratch_shapes=[
            pltpu.VMEM((block_count, padded, HD), bf16),
            pltpu.VMEM((block_count, padded, HD), bf16),
            pltpu.VMEM((padded, HD), bf16),
            pltpu.VMEM((size, padded), f32),
            pltpu.VMEM((size, padded), f32),
            pltpu.VMEM((2, size, HD), f32),
            pltpu.SemaphoreType.DMA((2, block_count)),
        ],
        compiler_params=pltpu.CompilerParams(vmem_limit_bytes=60 << 20),
        name="attend",
    )(bounds, blocks, places, *query_chunks, keys, values, fresh_keys, fresh_values)


def project(pieces, weight, heads):
    arrays = []
    where = []
    for chunk in pieces:
        for array, index in chunk:
            found = [n for n, a in enumerate(arrays) if a is array]
            if not found:
                arrays.append(array)
                found = [len(arrays) - 1]
            where.append((found[0], index))
    chunks = len(pieces)
    sources = len(pieces[0])
    rows = arrays[0].shape[1]
    width = heads * HD
    step = 512

    def body(*refs):
        held = refs[: len(arrays)]
        weight_ref = refs[len(arrays)]
        outs = refs[len(arrays) + 1 : len(arrays) + 1 + chunks]
        attention = refs[-1]

        @pl.when(pl.program_id(0) == 0)
        def _():
            for t in range(chunks):
                spots = where[t * sources : (t + 1) * sources]
                stats = [held[a][c, :, width:].astype(f32) for a, c in spots]
                for h in range(heads):
                    levels = [
                        s[:, h : h + 1] + s[:, h + heads : h + heads + 1] + s[:, h + 2 * heads : h + 2 * heads + 1]
                        for s in stats
                    ]
                    top = functools.reduce(jnp.maximum, levels)
                    shares = [jnp.exp2(level - top) for level in levels]
                    total = functools.reduce(jnp.add, shares)
                    mixed = None
                    for (a, c), share in zip(spots, shares):
                        term = held[a][c, :, h * HD : (h + 1) * HD].astype(f32) * share
                        mixed = term if mixed is None else mixed + term
                    attention[t * rows : (t + 1) * rows, h * HD : (h + 1) * HD] = (mixed / total).astype(bf16)

        result = jnp.dot(attention[...], weight_ref[...], preferred_element_type=f32).astype(bf16)
        for t in range(chunks):
            outs[t][...] = result[t * rows : (t + 1) * rows]

    whole = [pl.BlockSpec(a.shape, lambda n: (0, 0, 0)) for a in arrays]
    return pl.pallas_call(
        body,
        grid=(D // step,),
        in_specs=whole + [pl.BlockSpec((width, step), lambda n: (0, n))],
        out_specs=[pl.BlockSpec((rows, step), lambda n: (0, n))] * chunks,
        out_shape=[jax.ShapeDtypeStruct((rows, D), bf16)] * chunks,
        scratch_shapes=[pltpu.VMEM((chunks * rows, width), bf16)],
        name="project",
    )(*arrays, weight)


def normalize(residual, shares, gain, gates, experts):
    rows = residual.shape[0]

    def body(residual_ref, *refs):
        share_refs = refs[: len(shares)]
        gain_ref, gates_ref, hidden_ref, message_ref = refs[len(shares) :]
        hidden = share_refs[0][...].astype(f32)
        for ref in share_refs[1:]:
            hidden = hidden + ref[...].astype(f32)
        hidden = residual_ref[...].astype(f32) + hidden
        hidden_ref[...] = hidden
        power = jnp.mean(hidden * hidden, axis=-1, keepdims=True)
        message_ref[:, :D] = (hidden * lax.rsqrt(power + norm_epsilon) * gain_ref[...]).astype(bf16)
        if experts:
            first, second, third = three_parts(gates_ref[...])
            lane = lax.broadcasted_iota(jnp.int32, first.shape, 1)
            parts = jnp.where(lane < experts, first, jnp.where(lane < 2 * experts, second, third))
            message_ref[:, D:] = parts.astype(bf16)

    return pl.pallas_call(
        body,
        in_specs=[VM] * (len(shares) + 3),
        out_specs=[VM] * 2,
        out_shape=[
            jax.ShapeDtypeStruct((rows, D), f32),
            jax.ShapeDtypeStruct((rows, D + (HD if experts else 0)), bf16),
        ],
        name="normalize",
    )(residual, *shares, gain, gates)


def run_expert(expert, messages, gate_up, down, experts):
    rows = messages[0].shape[0]
    count = len(messages)
    step = 384
    steps = FF // step

    def body(expert_ref, *refs):
        message_refs = refs[:count]
        gate_ref, up_ref, down_ref, kept_ref, sent_ref, total = refs[count:]
        stage = pl.program_id(0)
        features = jnp.concatenate([ref[:, :D] for ref in message_refs], 0)
        gate = jnp.dot(features, gate_ref[...], preferred_element_type=f32)
        up = jnp.dot(features, up_ref[...], preferred_element_type=f32)
        inner = (gate / (1.0 + jnp.exp(-gate)) * up).astype(bf16)
        part = jnp.dot(inner, down_ref[...], preferred_element_type=f32)

        @pl.when(stage == 0)
        def _():
            total[...] = part

        @pl.when(stage > 0)
        def _():
            total[...] += part

        @pl.when(stage == steps - 1)
        def _():
            mine = expert_ref[0]
            lane = lax.broadcasted_iota(jnp.int32, (rows, HD), 1)
            chosen = (lane == mine) | (lane == mine + experts) | (lane == mine + 2 * experts)
            for c in range(count):
                parts = message_refs[c][:, D:].astype(f32)
                weight = jnp.sum(jnp.where(chosen, parts, 0.0), 1, keepdims=True)
                out = total[c * rows : (c + 1) * rows].astype(bf16).astype(f32) * weight
                if c < count // 2:
                    kept_ref[c * rows : (c + 1) * rows] = out
                else:
                    at = (c - count // 2) * rows
                    sent_ref[at : at + rows] = out.astype(bf16)

    whole = pl.BlockSpec((rows, D + HD), lambda n: (0, 0))
    half = count // 2 * rows
    return pl.pallas_call(
        body,
        grid=(steps,),
        in_specs=[SM]
        + [whole] * count
        + [
            pl.BlockSpec((D, step), lambda n: (0, n)),
            pl.BlockSpec((D, step), lambda n: (0, n + steps)),
            pl.BlockSpec((step, D), lambda n: (n, 0)),
        ],
        out_specs=[pl.BlockSpec((half, D), lambda n: (0, 0))] * 2,
        out_shape=[jax.ShapeDtypeStruct((half, D), f32), jax.ShapeDtypeStruct((half, D), bf16)],
        scratch_shapes=[pltpu.VMEM((count * rows, D), f32)],
        name="run_expert",
    )(expert, *messages, gate_up, gate_up, down)


def mix_all_rows(message, gate_up, down, experts):
    kv_count = lax.axis_size("kv")
    rows = message.shape[0]
    mine = (lax.axis_index("ep") * kv_count + lax.axis_index("kv")).reshape(1).astype(jnp.int32)
    total = None
    groups = []
    for k in range(kv_count):
        here = shifted(message, "kv", k)
        across = swapped(here, "ep", 2)
        groups.append((here, across, swapped(here, "ep", 1), swapped(across, "ep", 1)))
    for k, group in enumerate(groups):
        kept, sent = run_expert(mine, group, gate_up, down, experts)
        pair = kept + swapped(sent, "ep", 1).astype(f32)
        part = pair[:rows] + swapped(pair[rows:].astype(bf16), "ep", 2).astype(f32)
        if k:
            part = shifted(part.astype(bf16), "kv", -k).astype(f32)
        total = part if total is None else total + part
    return total


def mix_sent_rows(normed, gate_up, down, expert_ids, route_weights, capacity, experts):
    rows = normed.shape[0]
    pair_expert = expert_ids.reshape(-1)
    one_hot = (pair_expert[:, None] == jnp.arange(experts, dtype=jnp.int32)[None, :]).astype(jnp.int32)
    slot_index = jnp.sum((jnp.cumsum(one_hot, axis=0) - 1) * one_hot, axis=1)
    outbound = (
        jnp.zeros((experts, capacity, D), bf16).at[pair_expert, slot_index].set(jnp.repeat(normed, TOPK, axis=0))
    )
    received = lax.all_to_all(outbound, ("ep", "kv"), split_axis=0, concat_axis=0, tiled=True)
    sources, slots, width = received.shape
    mixed = jnp.dot(received.reshape(sources * slots, width), gate_up, preferred_element_type=f32)
    inner = (jax.nn.silu(mixed[:, :FF]) * mixed[:, FF:]).astype(bf16)
    outputs = jnp.dot(inner, down, preferred_element_type=f32).astype(bf16)
    returned = lax.all_to_all(
        outputs.reshape(sources, slots, width), ("ep", "kv"), split_axis=0, concat_axis=0, tiled=True
    )
    picked = returned[pair_expert, slot_index].reshape(rows, TOPK, D)
    return jnp.einsum("rk,rkd->rd", route_weights, picked.astype(f32))


def shards(
    queries,
    new_keys,
    new_values,
    key_cache,
    value_cache,
    lengths,
    residual_in,
    out_weight,
    norm_gain,
    gate_up_weight,
    down_weight,
    expert_ids,
    route_weights,
):
    kv_count = lax.axis_size("kv")
    kv_place = lax.axis_index("kv")
    ep_count = lax.axis_size("ep")
    experts = ep_count * kv_count
    rows = queries.shape[0]
    cached = key_cache.shape[1]
    heads = QH // kv_count
    assert key_cache.shape[0] == 1 and rows * kv_count == BLOCK

    near_first = sorted(range(kv_count), key=lambda c: min(c, kv_count - c))
    chunks = {c: shifted(queries, "kv", c) for c in near_first}
    bounds = jnp.stack([jnp.clip(lengths[0] - kv_place * cached, 0, cached), kv_place * rows]).astype(jnp.int32)
    blocks = (kv_place + 1 + jnp.arange(kv_count, dtype=jnp.int32)) % kv_count
    if kv_count == 4:
        calls = GROUPS
    else:
        calls = [near_first[at : at + 2] for at in range(0, kv_count, 2)]
    shares = {}
    for call in calls:
        places = jnp.stack([(kv_place - c) % kv_count for c in call]).astype(jnp.int32)
        outs = attend(
            bounds,
            blocks,
            places,
            [chunks[c] for c in call],
            key_cache[0],
            value_cache[0],
            new_keys,
            new_values,
            heads,
        )
        for k in range(kv_count):
            landed = shifted(outs[k - 1], "kv", k)
            for index, c in enumerate(call):
                shares[k, c] = (landed, index)
    pieces = [[shares[k, (t - k) % kv_count] for k in range(kv_count)] for t in range(kv_count)]
    projected = project(pieces, out_weight, heads)
    landed = [shifted(projected[t], "kv", -t) for t in range(kv_count)]

    capacity = min(rows, max(2, 2 * rows * TOPK // experts))
    everywhere = capacity == rows and ep_count == 4 and 3 * experts <= HD
    named = expert_ids[:, :, None] == jnp.arange(experts, dtype=jnp.int32)[None, None, :]
    gates = jnp.sum(jnp.where(named, route_weights[:, :, None], 0.0), axis=1)
    if everywhere:
        gates = jnp.pad(jnp.tile(gates, (1, 3)), ((0, 0), (0, HD - 3 * experts)))
    hidden_state, message = normalize(
        residual_in, landed, norm_gain[None], gates, experts if everywhere else 0
    )
    if everywhere:
        mixture = mix_all_rows(message, gate_up_weight[0], down_weight[0], experts)
    else:
        mixture = mix_sent_rows(
            message, gate_up_weight[0], down_weight[0], expert_ids, route_weights, capacity, experts
        )
    return (hidden_state + mixture).astype(bf16)


GROUPS = [[0], [1, 3], [2]]


def solution(mesh):
    placed = (
        P(("group", "ep", "kv"), None),
        P(("group", "ep", "kv"), None),
        P(("group", "ep", "kv"), None),
        P(("group", "ep"), "kv", None),
        P(("group", "ep"), "kv", None),
        P(("group", "ep")),
        P(("group", "ep", "kv"), None),
        P("kv", None),
        P(),
        P(("ep", "kv"), None, None),
        P(("ep", "kv"), None, None),
        P(("group", "ep", "kv"), None),
        P(("group", "ep", "kv"), None),
    )
    return jax.shard_map(
        shards,
        mesh=mesh,
        in_specs=placed,
        out_specs=P(("group", "ep", "kv"), None),
        check_vma=False,
    )
```

```python
import functools
import math

import jax
import jax.numpy as jnp
from jax import lax
from jax.experimental import pallas as pl
from jax.experimental.pallas import tpu as pltpu
from jax.sharding import PartitionSpec as P

D = 2048
QH = 32
KVH = 4
HD = 128
FF = 768
TOPK = 8
BLOCK = 128

absent = -1e30
masked_score = -3e38
norm_epsilon = 1e-06
score_scale = math.log2(math.e) * HD**-0.5
key_step = 512
row_step = 256
f32 = jnp.float32
bf16 = jnp.bfloat16

HBM = pl.BlockSpec(memory_space=pltpu.HBM)
VM = pl.BlockSpec(memory_space=pltpu.VMEM)
SM = pl.BlockSpec(memory_space=pltpu.SMEM)


def in_hbm(array):
    return pltpu.with_memory_space_constraint(array, pltpu.HBM)


def shifted(array, axis, by):
    size = lax.axis_size(axis)
    if by % size == 0:
        return array
    return lax.ppermute(array, axis, [(i, (i + by) % size) for i in range(size)])


def swapped(array, axis, bit):
    return lax.ppermute(array, axis, [(i, i ^ bit) for i in range(lax.axis_size(axis))])


def scored(left, right):
    return lax.dot_general(left, right, (((1,), (1,)), ((), ())), preferred_element_type=f32)


def three_parts(value):
    first = value.astype(bf16).astype(f32)
    rest = value - first
    second = rest.astype(bf16).astype(f32)
    return first, second, rest - second


def attend(bounds, blocks, places, query_chunks, keys, values, fresh_keys, fresh_values, heads, own_first):
    count = len(query_chunks)
    rows = query_chunks[0].shape[0]
    block_count = QH // heads
    per_key_head = QH // KVH // heads
    cached = keys.shape[0]
    fresh = fresh_keys.shape[0]
    padded = cached + 128
    width = heads * HD
    size = count * heads * rows

    def body(*refs):
        bounds_ref, blocks_ref, places_ref = refs[:3]
        query_refs = refs[3 : 3 + count]
        key_hbm, value_hbm, fresh_key_ref, fresh_value_ref = refs[3 + count : 7 + count]
        outs = refs[7 + count : 7 + count + block_count]
        keys_in, values_in, ones, even, odd, largest, result, fresh_in, own_in, sems, fresh_sems = refs[7 + count + block_count :]
        if own_first:
            own_copy = pltpu.make_async_copy(query_refs[0], own_in, fresh_sems.at[2])
            own_copy.start()
            query_refs = (own_in, *query_refs[1:])
        fresh_copies = [
            pltpu.make_async_copy(ref, fresh_in.at[n], fresh_sems.at[n])
            for n, ref in enumerate((fresh_key_ref, fresh_value_ref))
        ]
        for copy in fresh_copies:
            copy.start()
        score_refs = (even, odd)
        filled = bounds_ref[0]
        fresh_start = bounds_ref[1]

        def lane_of(i):
            return pl.multiple_of((blocks_ref[i] // per_key_head) * HD, HD)

        def key_copy(i):
            return pltpu.make_async_copy(
                key_hbm.at[:, pl.ds(lane_of(i), HD)], keys_in.at[i, pl.ds(0, cached)], sems.at[0, i]
            )

        def value_copy(i):
            return pltpu.make_async_copy(
                value_hbm.at[:, pl.ds(lane_of(i), HD)], values_in.at[i, pl.ds(0, cached)], sems.at[1, i]
            )

        key_copy(0).start()
        place = lax.broadcasted_iota(jnp.int32, (padded, HD), 0)
        counted = (place < filled) | ((place >= cached) & (place < cached + fresh))
        ones[...] = jnp.where(counted, 1.0, 0.0).astype(bf16)
        blank = jnp.zeros((128 - fresh, HD), bf16)
        for copy in fresh_copies:
            copy.wait()
        for i in range(block_count):
            lanes = pl.ds(lane_of(i), HD)
            keys_in[i, cached : cached + fresh] = fresh_in[0, :, lanes]
            keys_in[i, cached + fresh :] = blank
            values_in[i, cached : cached + fresh] = fresh_in[1, :, lanes]
            values_in[i, cached + fresh :] = blank
        if own_first:
            own_copy.wait()

        def replace_unfilled(ref, i, filler):
            @pl.when(filled < cached)
            def _():
                def one(block, carry):
                    at = pl.ds(pl.multiple_of(block * row_step, row_step), row_step)
                    inside = lax.broadcasted_iota(jnp.int32, (row_step, HD), 0) + block * row_step < filled
                    ref[i, at] = jnp.where(inside, ref[i, at], filler)
                    return carry

                lax.fori_loop(filled // row_step, cached // row_step, one, 0)

        def arrive_keys(i):
            key_copy(i).wait()
            replace_unfilled(keys_in, i, jnp.broadcast_to(keys_in[i, :1], (row_step, HD)))

        def arrive_values(i):
            value_copy(i).wait()
            replace_unfilled(values_in, i, jnp.zeros((row_step, HD), bf16))

        def fill_scores(i, slot):
            out = score_refs[slot]
            lanes = pl.ds(pl.multiple_of(blocks_ref[i] * width, HD), width)
            chunks = [ref[:, lanes].astype(f32) * score_scale for ref in query_refs]
            stacked = jnp.concatenate([c[:, h * HD : (h + 1) * HD] for c in chunks for h in range(heads)], 0)
            high = stacked.astype(bf16)
            both = jnp.concatenate([high, (stacked - high.astype(f32)).astype(bf16)], 1)
            running = None
            for start in range(0, cached, key_step):
                part = keys_in[i, start : start + key_step]
                scores = scored(both, jnp.concatenate([part, part], 1))
                out[:, start : start + key_step] = scores
                for at in range(0, key_step, HD):
                    piece = scores[:, at : at + HD]
                    running = piece if running is None else jnp.maximum(running, piece)
            part = keys_in[i, cached:]
            scores = scored(both, jnp.concatenate([part, part], 1))
            row = lax.broadcasted_iota(jnp.int32, (rows, HD), 0)
            column = lax.broadcasted_iota(jnp.int32, (rows, HD), 1)
            masked = []
            for c in range(count):
                seen = (column < fresh) & (column + fresh_start <= row + places_ref[c] * rows)
                own = scores[c * heads * rows : (c + 1) * heads * rows]
                masked.append(jnp.where(jnp.tile(seen, (heads, 1)), own, masked_score))
            scores = jnp.concatenate(masked, 0)
            out[:, cached:] = scores
            running = jnp.maximum(running, scores)
            top = jnp.maximum(jnp.max(running, 1, keepdims=True), absent)
            largest[slot] = jnp.broadcast_to(top, (size, HD))

        def weigh(i, slot):
            top = largest[slot]
            probs = jnp.exp2(score_refs[slot][...] - top[:, :1]).astype(bf16)
            both = jnp.concatenate([values_in[i], ones[...]], 1)
            total = jnp.dot(probs, both, preferred_element_type=f32)
            lane = lax.broadcasted_iota(jnp.int32, (rows, HD), 1)
            for c in range(count):
                stats = jnp.zeros((rows, HD), f32)
                for h in range(heads):
                    at = (c * heads + h) * rows
                    piece = total[at : at + rows]
                    norm = piece[:, HD:]
                    some = norm > 0
                    safe = jnp.where(some, norm, 1.0)
                    result[c, :, h * HD : (h + 1) * HD] = (piece[:, :HD] / safe).astype(bf16)
                    level = jnp.where(some, top[at : at + rows] + jnp.log2(safe), absent)
                    for k, part in enumerate(three_parts(level)):
                        stats = jnp.where(lane == h + k * heads, part, stats)
                result[c, :, width:] = stats.astype(bf16)
            for n in range(slot, block_count, 2):

                @pl.when(i == n)
                def _():
                    outs[n][...] = result[...]

        arrive_keys(0)
        for i in range(1, block_count):
            key_copy(i).start()
            value_copy(i - 1).start()
        value_copy(block_count - 1).start()
        fill_scores(0, 0)

        def pair(t, carry):
            arrive_keys(2 * t + 1)
            arrive_values(2 * t)
            fill_scores(2 * t + 1, 1)
            weigh(2 * t, 0)

            @pl.when(t < block_count // 2 - 1)
            def _():
                arrive_keys(2 * t + 2)
                arrive_values(2 * t + 1)
                fill_scores(2 * t + 2, 0)
                weigh(2 * t + 1, 1)

            return carry

        lax.fori_loop(0, block_count // 2, pair, 0)
        arrive_values(block_count - 1)
        weigh(block_count - 1, 1)

    return pl.pallas_call(
        body,
        in_specs=[SM] * 3 + [HBM if own_first and n == 0 else VM for n in range(count)] + [HBM] * 4,
        out_specs=[VM] * block_count,
        out_shape=[jax.ShapeDtypeStruct((count, rows, width + HD), bf16)] * block_count,
        scratch_shapes=[
            pltpu.VMEM((block_count, padded, HD), bf16),
            pltpu.VMEM((block_count, padded, HD), bf16),
            pltpu.VMEM((padded, HD), bf16),
            pltpu.VMEM((size, padded), f32),
            pltpu.VMEM((size, padded), f32),
            pltpu.VMEM((2, size, HD), f32),
            pltpu.VMEM((count, rows, width + HD), bf16),
            pltpu.VMEM((2, fresh, KVH * HD), bf16),
            pltpu.VMEM((rows, QH * HD), bf16),
            pltpu.SemaphoreType.DMA((2, block_count)),
            pltpu.SemaphoreType.DMA((3,)),
        ],
        compiler_params=pltpu.CompilerParams(vmem_limit_bytes=12 * size * padded + (16 << 20)),
        cost_estimate=pl.CostEstimate(
            flops=block_count * size * padded * HD * 2 * 16,
            transcendentals=block_count * size * padded,
            bytes_accessed=4 * cached * KVH * HD,
        ),
    )(
        bounds,
        blocks,
        places,
        *[in_hbm(c) if own_first and n == 0 else c for n, c in enumerate(query_chunks)],
        *[in_hbm(a) for a in (keys, values, fresh_keys, fresh_values)],
    )


def project(pieces, weight, heads):
    arrays = []
    where = []
    for chunk in pieces:
        for array, index in chunk:
            found = [n for n, a in enumerate(arrays) if a is array]
            if not found:
                arrays.append(array)
                found = [len(arrays) - 1]
            where.append((found[0], index))
    chunks = len(pieces)
    sources = len(pieces[0])
    rows = arrays[0].shape[1]
    width = heads * HD
    step = 512

    def body(*refs):
        held = refs[: len(arrays)]
        weight_ref = refs[len(arrays)]
        outs = refs[len(arrays) + 1 : len(arrays) + 1 + chunks]
        attention = refs[-1]

        @pl.when(pl.program_id(0) == 0)
        def _():
            for t in range(chunks):
                spots = where[t * sources : (t + 1) * sources]
                stats = [held[a][c, :, width:].astype(f32) for a, c in spots]
                for h in range(heads):
                    levels = [
                        s[:, h : h + 1] + s[:, h + heads : h + heads + 1] + s[:, h + 2 * heads : h + 2 * heads + 1]
                        for s in stats
                    ]
                    top = functools.reduce(jnp.maximum, levels)
                    shares = [jnp.exp2(level - top) for level in levels]
                    total = functools.reduce(jnp.add, shares)
                    mixed = None
                    for (a, c), share in zip(spots, shares):
                        term = held[a][c, :, h * HD : (h + 1) * HD].astype(f32) * share
                        mixed = term if mixed is None else mixed + term
                    attention[t * rows : (t + 1) * rows, h * HD : (h + 1) * HD] = (mixed / total).astype(bf16)

        result = jnp.dot(attention[...], weight_ref[...], preferred_element_type=f32).astype(bf16)
        for t in range(chunks):
            outs[t][...] = result[t * rows : (t + 1) * rows]

    return pl.pallas_call(
        body,
        grid=(D // step,),
        in_specs=[VM] * len(arrays) + [pl.BlockSpec((width, step), lambda n: (0, n))],
        out_specs=[pl.BlockSpec((rows, step), lambda n: (0, n))] * chunks,
        out_shape=[jax.ShapeDtypeStruct((rows, D), bf16)] * chunks,
        scratch_shapes=[pltpu.VMEM((chunks * rows, width), bf16)],
        name="project",
    )(*arrays, in_hbm(weight))


def normalize(residual, shares, gain, gates, experts):
    rows = residual.shape[0]

    def body(residual_ref, *refs):
        share_refs = refs[: len(shares)]
        gain_ref, gates_ref, hidden_ref, message_ref = refs[len(shares) :]
        hidden = share_refs[0][...].astype(f32)
        for ref in share_refs[1:]:
            hidden = hidden + ref[...].astype(f32)
        hidden = residual_ref[...].astype(f32) + hidden
        hidden_ref[...] = hidden
        power = jnp.mean(hidden * hidden, axis=-1, keepdims=True)
        message_ref[:, :D] = (hidden * lax.rsqrt(power + norm_epsilon) * gain_ref[...]).astype(bf16)
        if experts:
            first, second, third = three_parts(gates_ref[...])
            lane = lax.broadcasted_iota(jnp.int32, first.shape, 1)
            parts = jnp.where(lane < experts, first, jnp.where(lane < 2 * experts, second, third))
            message_ref[:, D:] = parts.astype(bf16)

    return pl.pallas_call(
        body,
        in_specs=[VM] * (len(shares) + 3),
        out_specs=[VM] * 2,
        out_shape=[
            jax.ShapeDtypeStruct((rows, D), f32),
            jax.ShapeDtypeStruct((rows, D + (HD if experts else 0)), bf16),
        ],
        name="normalize",
    )(residual, *shares, gain, gates)


def run_expert(expert, messages, gate_up, down, experts):
    rows = messages[0].shape[0]
    count = len(messages)
    half = count // 2 * rows
    step = 256
    steps = FF // step

    def body(expert_ref, *refs):
        message_refs = refs[:count]
        gate_ref, up_ref, down_ref, kept_ref, sent_ref, features, total = refs[count:]
        stage = pl.program_id(0)

        @pl.when(stage == 0)
        def _():
            for c in range(count):
                features[c * rows : (c + 1) * rows] = message_refs[c][:, :D]

        gate = jnp.dot(features[...], gate_ref[...], preferred_element_type=f32)
        up = jnp.dot(features[...], up_ref[...], preferred_element_type=f32)
        inner = (gate / (1.0 + jnp.exp(-gate)) * up).astype(bf16)

        part = jnp.dot(inner, down_ref[...], preferred_element_type=f32)

        @pl.when(stage == 0)
        def _():
            total[...] = part

        @pl.when(stage > 0)
        def _():
            total[...] += part

        @pl.when(stage == steps - 1)
        def _():
            mine = expert_ref[0]
            lane = lax.broadcasted_iota(jnp.int32, (rows, HD), 1)
            chosen = (lane == mine) | (lane == mine + experts) | (lane == mine + 2 * experts)
            for c in range(count):
                parts = message_refs[c][:, D:].astype(f32)
                weight = jnp.sum(jnp.where(chosen, parts, 0.0), 1, keepdims=True)
                out = total[c * rows : (c + 1) * rows].astype(bf16).astype(f32) * weight
                if c < count // 2:
                    kept_ref[c * rows : (c + 1) * rows] = out
                else:
                    at = c * rows - half
                    sent_ref[at : at + rows] = out.astype(bf16)

    return pl.pallas_call(
        body,
        grid=(steps,),
        in_specs=[SM]
        + [VM] * count
        + [
            pl.BlockSpec((D, step), lambda n: (0, n)),
            pl.BlockSpec((D, step), lambda n: (0, n + steps)),
            pl.BlockSpec((step, D), lambda n: (n, 0)),
        ],
        out_specs=[VM] * 2,
        out_shape=[jax.ShapeDtypeStruct((half, D), f32), jax.ShapeDtypeStruct((half, D), bf16)],
        scratch_shapes=[pltpu.VMEM((count * rows, D), bf16), pltpu.VMEM((count * rows, D), f32)],
        compiler_params=pltpu.CompilerParams(vmem_limit_bytes=36 << 20),
        name="run_expert",
    )(expert, *messages, in_hbm(gate_up), in_hbm(gate_up), in_hbm(down))


def mix_all_rows(message, gate_up, down, experts):
    kv_count = lax.axis_size("kv")
    rows = message.shape[0]
    mine = (lax.axis_index("ep") * kv_count + lax.axis_index("kv")).reshape(1).astype(jnp.int32)
    order = sorted(range(kv_count), key=lambda c: -min(c, kv_count - c))
    here = {k: shifted(message, "kv", k) for k in order}
    across = {k: swapped(here[k], "ep", 2) for k in reversed(order)}
    own = [here[k] for k in order] + [across[k] for k in order]
    paired = {m: swapped(own[m], "ep", 1) for m in reversed(range(len(own)))}
    kept, sent = run_expert(mine, own + [paired[m] for m in range(len(own))], gate_up, down, experts)
    pair = kept + swapped(sent, "ep", 1).astype(f32)
    total = None
    for n, k in enumerate(order):
        at = n * rows
        far = at + kv_count * rows
        part = pair[at : at + rows] + swapped(pair[far : far + rows].astype(bf16), "ep", 2).astype(f32)
        if k:
            part = shifted(part.astype(bf16), "kv", -k).astype(f32)
        total = part if total is None else total + part
    return total


def mix_sent_rows(normed, gate_up, down, expert_ids, route_weights, capacity, experts):
    rows = normed.shape[0]
    pair_expert = expert_ids.reshape(-1)
    one_hot = (pair_expert[:, None] == jnp.arange(experts, dtype=jnp.int32)[None, :]).astype(jnp.int32)
    slot_index = jnp.sum((jnp.cumsum(one_hot, axis=0) - 1) * one_hot, axis=1)
    outbound = (
        jnp.zeros((experts, capacity, D), bf16).at[pair_expert, slot_index].set(jnp.repeat(normed, TOPK, axis=0))
    )
    received = lax.all_to_all(outbound, ("ep", "kv"), split_axis=0, concat_axis=0, tiled=True)
    sources, slots, width = received.shape
    mixed = jnp.dot(received.reshape(sources * slots, width), gate_up, preferred_element_type=f32)
    inner = (jax.nn.silu(mixed[:, :FF]) * mixed[:, FF:]).astype(bf16)
    outputs = jnp.dot(inner, down, preferred_element_type=f32).astype(bf16)
    returned = lax.all_to_all(
        outputs.reshape(sources, slots, width), ("ep", "kv"), split_axis=0, concat_axis=0, tiled=True
    )
    picked = returned[pair_expert, slot_index].reshape(rows, TOPK, D)
    return jnp.einsum("rk,rkd->rd", route_weights, picked.astype(f32))


def shards(
    queries,
    new_keys,
    new_values,
    key_cache,
    value_cache,
    lengths,
    residual_in,
    out_weight,
    norm_gain,
    gate_up_weight,
    down_weight,
    expert_ids,
    route_weights,
):
    kv_count = lax.axis_size("kv")
    kv_place = lax.axis_index("kv")
    ep_count = lax.axis_size("ep")
    experts = ep_count * kv_count
    rows = queries.shape[0]
    cached = key_cache.shape[1]
    heads = QH // kv_count
    assert key_cache.shape[0] == 1 and rows * kv_count == BLOCK

    near_first = sorted(range(kv_count), key=lambda c: min(c, kv_count - c))
    chunks = {c: shifted(queries, "kv", c) for c in near_first}
    bounds = jnp.stack([jnp.clip(lengths[0] - kv_place * cached, 0, cached), kv_place * rows]).astype(jnp.int32)
    blocks = (kv_place + 1 + jnp.arange(kv_count, dtype=jnp.int32)) % kv_count
    if kv_count == 4:
        calls = GROUPS
    else:
        calls = [near_first[at : at + 2] for at in range(0, kv_count, 2)]
    shares = {}

    def send(k, outs, call):
        landed = shifted(outs[k - 1], "kv", k)
        for index, c in enumerate(call):
            shares[k, c] = (landed, index)

    outs = None
    for call in calls:
        places = jnp.stack([(kv_place - c) % kv_count for c in call]).astype(jnp.int32)
        if outs is not None:
            places, *outs = lax.optimization_barrier((places, *outs))
            for k in range(kv_count):
                send(k, outs, before)
        outs = attend(
            bounds,
            blocks,
            places,
            [chunks[c] for c in call],
            key_cache[0],
            value_cache[0],
            new_keys,
            new_values,
            heads,
            0 in call,
        )
        before = call
    for k in range(kv_count):
        send(k, outs, before)
    pieces = [[shares[k, (t - k) % kv_count] for k in range(kv_count)] for t in range(kv_count)]
    projected = project(pieces, out_weight, heads)
    landed = [shifted(projected[t], "kv", -t) for t in range(kv_count)]

    capacity = min(rows, max(2, 2 * rows * TOPK // experts))
    everywhere = capacity == rows and ep_count == 4 and kv_count == 4 and 3 * experts <= HD
    named = expert_ids[:, :, None] == jnp.arange(experts, dtype=jnp.int32)[None, None, :]
    gates = jnp.sum(jnp.where(named, route_weights[:, :, None], 0.0), axis=1)
    if everywhere:
        gates = jnp.pad(jnp.tile(gates, (1, 3)), ((0, 0), (0, HD - 3 * experts)))
    hidden_state, message = normalize(
        residual_in, landed, norm_gain[None], gates, experts if everywhere else 0
    )
    if everywhere:
        mixture = mix_all_rows(message, gate_up_weight[0], down_weight[0], experts)
    else:
        mixture = mix_sent_rows(
            message, gate_up_weight[0], down_weight[0], expert_ids, route_weights, capacity, experts
        )
    return (hidden_state + mixture).astype(bf16)


GROUPS = [[0], [1, 3], [2]]


def solution(mesh):
    placed = (
        P(("group", "ep", "kv"), None),
        P(("group", "ep", "kv"), None),
        P(("group", "ep", "kv"), None),
        P(("group", "ep"), "kv", None),
        P(("group", "ep"), "kv", None),
        P(("group", "ep")),
        P(("group", "ep", "kv"), None),
        P("kv", None),
        P(),
        P(("ep", "kv"), None, None),
        P(("ep", "kv"), None, None),
        P(("group", "ep", "kv"), None),
        P(("group", "ep", "kv"), None),
    )
    return jax.shard_map(
        shards,
        mesh=mesh,
        in_specs=placed,
        out_specs=P(("group", "ep", "kv"), None),
        check_vma=False,
    )
```

```python
import functools
import math

import jax
import jax.numpy as jnp
from jax import lax
from jax.experimental import pallas as pl
from jax.experimental.pallas import tpu as pltpu
from jax.sharding import PartitionSpec as P

D = 2048
QH = 32
KVH = 4
HD = 128
FF = 768
TOPK = 8
BLOCK = 128

absent = -1e30
masked_score = -3e38
norm_epsilon = 1e-06
score_scale = math.log2(math.e) * HD**-0.5
key_step = 512
row_step = 256
f32 = jnp.float32
bf16 = jnp.bfloat16

HBM = pl.BlockSpec(memory_space=pltpu.HBM)
VM = pl.BlockSpec(memory_space=pltpu.VMEM)
SM = pl.BlockSpec(memory_space=pltpu.SMEM)


def in_hbm(array):
    return pltpu.with_memory_space_constraint(array, pltpu.HBM)


def shifted(array, axis, by):
    size = lax.axis_size(axis)
    if by % size == 0:
        return array
    return lax.ppermute(array, axis, [(i, (i + by) % size) for i in range(size)])


def swapped(array, axis, bit):
    return lax.ppermute(array, axis, [(i, i ^ bit) for i in range(lax.axis_size(axis))])


def scored(left, right):
    return lax.dot_general(left, right, (((1,), (1,)), ((), ())), preferred_element_type=f32)


def three_parts(value):
    first = value.astype(bf16).astype(f32)
    rest = value - first
    second = rest.astype(bf16).astype(f32)
    return first, second, rest - second


def attend(bounds, blocks, places, query_chunks, keys, values, fresh_keys, fresh_values, heads, own_first):
    count = len(query_chunks)
    rows = query_chunks[0].shape[0]
    block_count = QH // heads
    per_key_head = QH // KVH // heads
    cached = keys.shape[0]
    fresh = fresh_keys.shape[0]
    padded = cached + 128
    width = heads * HD
    size = count * heads * rows

    def body(*refs):
        bounds_ref, blocks_ref, places_ref = refs[:3]
        query_refs = refs[3 : 3 + count]
        key_hbm, value_hbm, fresh_key_ref, fresh_value_ref = refs[3 + count : 7 + count]
        outs = refs[7 + count : 7 + count + block_count]
        keys_in, values_in, ones, even, odd, largest, result, fresh_in, own_in, sems, fresh_sems = refs[7 + count + block_count :]
        if own_first:
            own_copy = pltpu.make_async_copy(query_refs[0], own_in, fresh_sems.at[2])
            own_copy.start()
            query_refs = (own_in, *query_refs[1:])
        fresh_copies = [
            pltpu.make_async_copy(ref, fresh_in.at[n], fresh_sems.at[n])
            for n, ref in enumerate((fresh_key_ref, fresh_value_ref))
        ]
        for copy in fresh_copies:
            copy.start()
        score_refs = (even, odd)
        filled = bounds_ref[0]
        fresh_start = bounds_ref[1]

        def lane_of(i):
            return pl.multiple_of((blocks_ref[i] // per_key_head) * HD, HD)

        def key_copy(i):
            return pltpu.make_async_copy(
                key_hbm.at[:, pl.ds(lane_of(i), HD)], keys_in.at[i, pl.ds(0, cached)], sems.at[0, i]
            )

        def value_copy(i):
            return pltpu.make_async_copy(
                value_hbm.at[:, pl.ds(lane_of(i), HD)], values_in.at[i, pl.ds(0, cached)], sems.at[1, i]
            )

        key_copy(0).start()
        place = lax.broadcasted_iota(jnp.int32, (padded, HD), 0)
        counted = (place < filled) | ((place >= cached) & (place < cached + fresh))
        ones[...] = jnp.where(counted, 1.0, 0.0).astype(bf16)
        blank = jnp.zeros((128 - fresh, HD), bf16)
        for copy in fresh_copies:
            copy.wait()
        for i in range(block_count):
            lanes = pl.ds(lane_of(i), HD)
            keys_in[i, cached : cached + fresh] = fresh_in[0, :, lanes]
            keys_in[i, cached + fresh :] = blank
            values_in[i, cached : cached + fresh] = fresh_in[1, :, lanes]
            values_in[i, cached + fresh :] = blank
        if own_first:
            own_copy.wait()

        def replace_unfilled(ref, i, filler):
            @pl.when(filled < cached)
            def _():
                def one(block, carry):
                    at = pl.ds(pl.multiple_of(block * row_step, row_step), row_step)
                    inside = lax.broadcasted_iota(jnp.int32, (row_step, HD), 0) + block * row_step < filled
                    ref[i, at] = jnp.where(inside, ref[i, at], filler)
                    return carry

                lax.fori_loop(filled // row_step, cached // row_step, one, 0)

        def arrive_keys(i):
            key_copy(i).wait()
            replace_unfilled(keys_in, i, jnp.broadcast_to(keys_in[i, :1], (row_step, HD)))

        def arrive_values(i):
            value_copy(i).wait()
            replace_unfilled(values_in, i, jnp.zeros((row_step, HD), bf16))

        def fill_scores(i, slot):
            out = score_refs[slot]
            lanes = pl.ds(pl.multiple_of(blocks_ref[i] * width, HD), width)
            chunks = [ref[:, lanes].astype(f32) * score_scale for ref in query_refs]
            stacked = jnp.concatenate([c[:, h * HD : (h + 1) * HD] for c in chunks for h in range(heads)], 0)
            high = stacked.astype(bf16)
            both = jnp.concatenate([high, (stacked - high.astype(f32)).astype(bf16)], 1)
            running = None
            for start in range(0, cached, key_step):
                part = keys_in[i, start : start + key_step]
                scores = scored(both, jnp.concatenate([part, part], 1))
                out[:, start : start + key_step] = scores
                for at in range(0, key_step, HD):
                    piece = scores[:, at : at + HD]
                    running = piece if running is None else jnp.maximum(running, piece)
            part = keys_in[i, cached:]
            scores = scored(both, jnp.concatenate([part, part], 1))
            row = lax.broadcasted_iota(jnp.int32, (rows, HD), 0)
            column = lax.broadcasted_iota(jnp.int32, (rows, HD), 1)
            masked = []
            for c in range(count):
                seen = (column < fresh) & (column + fresh_start <= row + places_ref[c] * rows)
                own = scores[c * heads * rows : (c + 1) * heads * rows]
                masked.append(jnp.where(jnp.tile(seen, (heads, 1)), own, masked_score))
            scores = jnp.concatenate(masked, 0)
            out[:, cached:] = scores
            running = jnp.maximum(running, scores)
            top = jnp.maximum(jnp.max(running, 1, keepdims=True), absent)
            largest[slot] = jnp.broadcast_to(top, (size, HD))

        def weigh(i, slot):
            top = largest[slot]
            probs = jnp.exp2(score_refs[slot][...] - top[:, :1]).astype(bf16)
            both = jnp.concatenate([values_in[i], ones[...]], 1)
            total = jnp.dot(probs, both, preferred_element_type=f32)
            lane = lax.broadcasted_iota(jnp.int32, (rows, HD), 1)
            for c in range(count):
                stats = jnp.zeros((rows, HD), f32)
                for h in range(heads):
                    at = (c * heads + h) * rows
                    piece = total[at : at + rows]
                    norm = piece[:, HD:]
                    some = norm > 0
                    safe = jnp.where(some, norm, 1.0)
                    result[c, :, h * HD : (h + 1) * HD] = (piece[:, :HD] / safe).astype(bf16)
                    level = jnp.where(some, top[at : at + rows] + jnp.log2(safe), absent)
                    for k, part in enumerate(three_parts(level)):
                        stats = jnp.where(lane == h + k * heads, part, stats)
                result[c, :, width:] = stats.astype(bf16)
            for n in range(slot, block_count, 2):

                @pl.when(i == n)
                def _():
                    outs[n][...] = result[...]

        arrive_keys(0)
        for i in range(1, block_count):
            key_copy(i).start()
            value_copy(i - 1).start()
        value_copy(block_count - 1).start()
        fill_scores(0, 0)

        def pair(t, carry):
            arrive_keys(2 * t + 1)
            arrive_values(2 * t)
            fill_scores(2 * t + 1, 1)
            weigh(2 * t, 0)

            @pl.when(t < block_count // 2 - 1)
            def _():
                arrive_keys(2 * t + 2)
                arrive_values(2 * t + 1)
                fill_scores(2 * t + 2, 0)
                weigh(2 * t + 1, 1)

            return carry

        lax.fori_loop(0, block_count // 2, pair, 0)
        arrive_values(block_count - 1)
        weigh(block_count - 1, 1)

    return pl.pallas_call(
        body,
        in_specs=[SM] * 3 + [HBM if own_first and n == 0 else VM for n in range(count)] + [HBM] * 4,
        out_specs=[VM] * block_count,
        out_shape=[jax.ShapeDtypeStruct((count, rows, width + HD), bf16)] * block_count,
        scratch_shapes=[
            pltpu.VMEM((block_count, padded, HD), bf16),
            pltpu.VMEM((block_count, padded, HD), bf16),
            pltpu.VMEM((padded, HD), bf16),
            pltpu.VMEM((size, padded), f32),
            pltpu.VMEM((size, padded), f32),
            pltpu.VMEM((2, size, HD), f32),
            pltpu.VMEM((count, rows, width + HD), bf16),
            pltpu.VMEM((2, fresh, KVH * HD), bf16),
            pltpu.VMEM((rows, QH * HD), bf16),
            pltpu.SemaphoreType.DMA((2, block_count)),
            pltpu.SemaphoreType.DMA((3,)),
        ],
        compiler_params=pltpu.CompilerParams(vmem_limit_bytes=12 * size * padded + (16 << 20)),
        cost_estimate=pl.CostEstimate(
            flops=block_count * size * padded * HD * 2 * 16,
            transcendentals=block_count * size * padded,
            bytes_accessed=4 * cached * KVH * HD,
        ),
    )(
        bounds,
        blocks,
        places,
        *[in_hbm(c) if own_first and n == 0 else c for n, c in enumerate(query_chunks)],
        *[in_hbm(a) for a in (keys, values, fresh_keys, fresh_values)],
    )


def project(pieces, weight, heads):
    arrays = []
    where = []
    for chunk in pieces:
        for array, index in chunk:
            found = [n for n, a in enumerate(arrays) if a is array]
            if not found:
                arrays.append(array)
                found = [len(arrays) - 1]
            where.append((found[0], index))
    chunks = len(pieces)
    sources = len(pieces[0])
    rows = arrays[0].shape[1]
    width = heads * HD
    step = 512

    def body(*refs):
        held = refs[: len(arrays)]
        weight_ref = refs[len(arrays)]
        outs = refs[len(arrays) + 1 : len(arrays) + 1 + chunks]
        attention = refs[-1]

        @pl.when(pl.program_id(0) == 0)
        def _():
            for t in range(chunks):
                spots = where[t * sources : (t + 1) * sources]
                stats = [held[a][c, :, width:].astype(f32) for a, c in spots]
                for h in range(heads):
                    levels = [
                        s[:, h : h + 1] + s[:, h + heads : h + heads + 1] + s[:, h + 2 * heads : h + 2 * heads + 1]
                        for s in stats
                    ]
                    top = functools.reduce(jnp.maximum, levels)
                    shares = [jnp.exp2(level - top) for level in levels]
                    total = functools.reduce(jnp.add, shares)
                    mixed = None
                    for (a, c), share in zip(spots, shares):
                        term = held[a][c, :, h * HD : (h + 1) * HD].astype(f32) * share
                        mixed = term if mixed is None else mixed + term
                    attention[t * rows : (t + 1) * rows, h * HD : (h + 1) * HD] = (mixed / total).astype(bf16)

        result = jnp.dot(attention[...], weight_ref[...], preferred_element_type=f32).astype(bf16)
        for t in range(chunks):
            outs[t][...] = result[t * rows : (t + 1) * rows]

    return pl.pallas_call(
        body,
        grid=(D // step,),
        in_specs=[VM] * len(arrays) + [pl.BlockSpec((width, step), lambda n: (0, n))],
        out_specs=[pl.BlockSpec((rows, step), lambda n: (0, n))] * chunks,
        out_shape=[jax.ShapeDtypeStruct((rows, D), bf16)] * chunks,
        scratch_shapes=[pltpu.VMEM((chunks * rows, width), bf16)],
        name="project",
    )(*arrays, in_hbm(weight))


def normalize(residual, shares, gain, gates, experts):
    rows = residual.shape[0]

    def body(residual_ref, *refs):
        share_refs = refs[: len(shares)]
        gain_ref, gates_ref, hidden_ref, message_ref = refs[len(shares) :]
        hidden = share_refs[0][...].astype(f32)
        for ref in share_refs[1:]:
            hidden = hidden + ref[...].astype(f32)
        hidden = residual_ref[...].astype(f32) + hidden
        hidden_ref[...] = hidden
        power = jnp.mean(hidden * hidden, axis=-1, keepdims=True)
        message_ref[:, :D] = (hidden * lax.rsqrt(power + norm_epsilon) * gain_ref[...]).astype(bf16)
        if experts:
            first, second, third = three_parts(gates_ref[...])
            lane = lax.broadcasted_iota(jnp.int32, first.shape, 1)
            parts = jnp.where(lane < experts, first, jnp.where(lane < 2 * experts, second, third))
            message_ref[:, D:] = parts.astype(bf16)

    return pl.pallas_call(
        body,
        in_specs=[VM] * (len(shares) + 3),
        out_specs=[VM] * 2,
        out_shape=[
            jax.ShapeDtypeStruct((rows, D), f32),
            jax.ShapeDtypeStruct((rows, D + (HD if experts else 0)), bf16),
        ],
        name="normalize",
    )(residual, *shares, gain, gates)


def run_expert(expert, messages, gate_up, down, experts):
    rows = messages[0].shape[0]
    count = len(messages)
    half = count // 2 * rows
    step = 256
    steps = FF // step

    def body(expert_ref, *refs):
        message_refs = refs[:count]
        gate_ref, up_ref, down_ref, kept_ref, sent_ref, features, total = refs[count:]
        stage = pl.program_id(0)

        @pl.when(stage == 0)
        def _():
            for c in range(count):
                features[c * rows : (c + 1) * rows] = message_refs[c][:, :D]

        gate = jnp.dot(features[...], gate_ref[...], preferred_element_type=f32)
        up = jnp.dot(features[...], up_ref[...], preferred_element_type=f32)
        inner = (gate / (1.0 + jnp.exp(-gate)) * up).astype(bf16)

        part = jnp.dot(inner, down_ref[...], preferred_element_type=f32)

        @pl.when(stage == 0)
        def _():
            total[...] = part

        @pl.when(stage > 0)
        def _():
            total[...] += part

        @pl.when(stage == steps - 1)
        def _():
            mine = expert_ref[0]
            lane = lax.broadcasted_iota(jnp.int32, (rows, HD), 1)
            chosen = (lane == mine) | (lane == mine + experts) | (lane == mine + 2 * experts)
            for c in range(count):
                parts = message_refs[c][:, D:].astype(f32)
                weight = jnp.sum(jnp.where(chosen, parts, 0.0), 1, keepdims=True)
                out = total[c * rows : (c + 1) * rows].astype(bf16).astype(f32) * weight
                if c < count // 2:
                    kept_ref[c * rows : (c + 1) * rows] = out
                else:
                    at = c * rows - half
                    sent_ref[at : at + rows] = out.astype(bf16)

    return pl.pallas_call(
        body,
        grid=(steps,),
        in_specs=[SM]
        + [VM] * count
        + [
            pl.BlockSpec((D, step), lambda n: (0, n)),
            pl.BlockSpec((D, step), lambda n: (0, n + steps)),
            pl.BlockSpec((step, D), lambda n: (n, 0)),
        ],
        out_specs=[VM] * 2,
        out_shape=[jax.ShapeDtypeStruct((half, D), f32), jax.ShapeDtypeStruct((half, D), bf16)],
        scratch_shapes=[pltpu.VMEM((count * rows, D), bf16), pltpu.VMEM((count * rows, D), f32)],
        compiler_params=pltpu.CompilerParams(vmem_limit_bytes=36 << 20),
        name="run_expert",
    )(expert, *messages, in_hbm(gate_up), in_hbm(gate_up), in_hbm(down))


def mix_all_rows(message, gate_up, down, experts):
    kv_count = lax.axis_size("kv")
    rows = message.shape[0]
    mine = (lax.axis_index("ep") * kv_count + lax.axis_index("kv")).reshape(1).astype(jnp.int32)
    order = sorted(range(kv_count), key=lambda c: -min(c, kv_count - c))
    here = {k: shifted(message, "kv", k) for k in order}
    across = {k: swapped(here[k], "ep", 2) for k in reversed(order)}
    own = [here[k] for k in order] + [across[k] for k in order]
    paired = {m: swapped(own[m], "ep", 1) for m in reversed(range(len(own)))}
    kept, sent = run_expert(mine, own + [paired[m] for m in range(len(own))], gate_up, down, experts)
    pair = kept + swapped(sent, "ep", 1).astype(f32)
    total = None
    for n, k in enumerate(order):
        at = n * rows
        far = at + kv_count * rows
        part = pair[at : at + rows] + swapped(pair[far : far + rows].astype(bf16), "ep", 2).astype(f32)
        if k:
            part = shifted(part.astype(bf16), "kv", -k).astype(f32)
        total = part if total is None else total + part
    return total


def mix_sent_rows(normed, gate_up, down, expert_ids, route_weights, capacity, experts):
    rows = normed.shape[0]
    pair_expert = expert_ids.reshape(-1)
    one_hot = (pair_expert[:, None] == jnp.arange(experts, dtype=jnp.int32)[None, :]).astype(jnp.int32)
    slot_index = jnp.sum((jnp.cumsum(one_hot, axis=0) - 1) * one_hot, axis=1)
    outbound = (
        jnp.zeros((experts, capacity, D), bf16).at[pair_expert, slot_index].set(jnp.repeat(normed, TOPK, axis=0))
    )
    received = lax.all_to_all(outbound, ("ep", "kv"), split_axis=0, concat_axis=0, tiled=True)
    sources, slots, width = received.shape
    mixed = jnp.dot(received.reshape(sources * slots, width), gate_up, preferred_element_type=f32)
    inner = (jax.nn.silu(mixed[:, :FF]) * mixed[:, FF:]).astype(bf16)
    outputs = jnp.dot(inner, down, preferred_element_type=f32).astype(bf16)
    returned = lax.all_to_all(
        outputs.reshape(sources, slots, width), ("ep", "kv"), split_axis=0, concat_axis=0, tiled=True
    )
    picked = returned[pair_expert, slot_index].reshape(rows, TOPK, D)
    return jnp.einsum("rk,rkd->rd", route_weights, picked.astype(f32))


def shards(
    queries,
    new_keys,
    new_values,
    key_cache,
    value_cache,
    lengths,
    residual_in,
    out_weight,
    norm_gain,
    gate_up_weight,
    down_weight,
    expert_ids,
    route_weights,
):
    kv_count = lax.axis_size("kv")
    kv_place = lax.axis_index("kv")
    ep_count = lax.axis_size("ep")
    experts = ep_count * kv_count
    rows = queries.shape[0]
    cached = key_cache.shape[1]
    heads = QH // kv_count
    assert key_cache.shape[0] == 1 and rows * kv_count == BLOCK

    near_first = sorted(range(kv_count), key=lambda c: min(c, kv_count - c))
    chunks = {}
    waiting = queries
    for c in near_first:
        distance = min(c, kv_count - c)
        if distance == 2:
            waiting = lax.optimization_barrier((queries, chunks[1], chunks[kv_count - 1]))[0]
        chunks[c] = shifted(waiting, "kv", c)
    bounds = jnp.stack([jnp.clip(lengths[0] - kv_place * cached, 0, cached), kv_place * rows]).astype(jnp.int32)
    blocks = (kv_place + 1 + jnp.arange(kv_count, dtype=jnp.int32)) % kv_count
    if kv_count == 4:
        calls = GROUPS
    else:
        calls = [near_first[at : at + 2] for at in range(0, kv_count, 2)]
    shares = {}

    def send(outs, call):
        landed = [shifted(outs[k - 1], "kv", k) for k in range(kv_count)]
        for k in range(kv_count):
            for index, c in enumerate(call):
                shares[k, c] = (landed[k], index)
        return landed

    outs = None
    sent = []
    for call in calls:
        places = jnp.stack([(kv_place - c) % kv_count for c in call]).astype(jnp.int32)
        if outs is not None:
            places, outs, sent = lax.optimization_barrier((places, outs, sent))
            for k, landed in enumerate(sent):
                for index, c in enumerate(earlier):
                    shares[k, c] = (landed, index)
            sent = send(outs, before)
            earlier = before
        outs = attend(
            bounds,
            blocks,
            places,
            [chunks[c] for c in call],
            key_cache[0],
            value_cache[0],
            new_keys,
            new_values,
            heads,
            0 in call,
        )
        before = call
    send(outs, before)
    pieces = [[shares[k, (t - k) % kv_count] for k in range(kv_count)] for t in range(kv_count)]
    projected = project(pieces, out_weight, heads)
    landed = [shifted(projected[t], "kv", -t) for t in range(kv_count)]

    capacity = min(rows, max(2, 2 * rows * TOPK // experts))
    everywhere = capacity == rows and ep_count == 4 and kv_count == 4 and 3 * experts <= HD
    named = expert_ids[:, :, None] == jnp.arange(experts, dtype=jnp.int32)[None, None, :]
    gates = jnp.sum(jnp.where(named, route_weights[:, :, None], 0.0), axis=1)
    if everywhere:
        gates = jnp.pad(jnp.tile(gates, (1, 3)), ((0, 0), (0, HD - 3 * experts)))
    hidden_state, message = normalize(
        residual_in, landed, norm_gain[None], gates, experts if everywhere else 0
    )
    if everywhere:
        mixture = mix_all_rows(message, gate_up_weight[0], down_weight[0], experts)
    else:
        mixture = mix_sent_rows(
            message, gate_up_weight[0], down_weight[0], expert_ids, route_weights, capacity, experts
        )
    return (hidden_state + mixture).astype(bf16)


GROUPS = [[0], [1, 3], [2]]


def solution(mesh):
    placed = (
        P(("group", "ep", "kv"), None),
        P(("group", "ep", "kv"), None),
        P(("group", "ep", "kv"), None),
        P(("group", "ep"), "kv", None),
        P(("group", "ep"), "kv", None),
        P(("group", "ep")),
        P(("group", "ep", "kv"), None),
        P("kv", None),
        P(),
        P(("ep", "kv"), None, None),
        P(("ep", "kv"), None, None),
        P(("group", "ep", "kv"), None),
        P(("group", "ep", "kv"), None),
    )
    return jax.shard_map(
        shards,
        mesh=mesh,
        in_specs=placed,
        out_specs=P(("group", "ep", "kv"), None),
        check_vma=False,
    )
```

```python
import functools
import math

import jax
import jax.numpy as jnp
from jax import lax
from jax.experimental import pallas as pl
from jax.experimental.pallas import tpu as pltpu
from jax.sharding import PartitionSpec as P

D = 2048
QH = 32
KVH = 4
HD = 128
FF = 768
TOPK = 8
BLOCK = 128

absent = -1e30
masked_score = -3e38
norm_epsilon = 1e-06
score_scale = math.log2(math.e) * HD**-0.5
key_step = 512
f32 = jnp.float32
bf16 = jnp.bfloat16

HBM = pl.BlockSpec(memory_space=pltpu.HBM)
VM = pl.BlockSpec(memory_space=pltpu.VMEM)
SM = pl.BlockSpec(memory_space=pltpu.SMEM)


def in_hbm(array):
    return pltpu.with_memory_space_constraint(array, pltpu.HBM)


def shifted(array, axis, by):
    size = lax.axis_size(axis)
    if by % size == 0:
        return array
    return lax.ppermute(array, axis, [(i, (i + by) % size) for i in range(size)])


def swapped(array, axis, bit):
    return lax.ppermute(array, axis, [(i, i ^ bit) for i in range(lax.axis_size(axis))])


def scored(left, right):
    return lax.dot_general(left, right, (((1,), (1,)), ((), ())), preferred_element_type=f32)


def three_parts(value):
    first = value.astype(bf16).astype(f32)
    rest = value - first
    second = rest.astype(bf16).astype(f32)
    return first, second, rest - second


def attend(bounds, blocks, places, query_chunks, keys, values, fresh_keys, fresh_values, heads, own_first):
    count = len(query_chunks)
    rows = query_chunks[0].shape[0]
    block_count = QH // heads
    per_key_head = QH // KVH // heads
    cached = keys.shape[0]
    fresh = fresh_keys.shape[0]
    padded = cached + 128
    width = heads * HD
    size = count * heads * rows

    def body(*refs):
        bounds_ref, blocks_ref, places_ref = refs[:3]
        query_refs = refs[3 : 3 + count]
        key_hbm, value_hbm, fresh_key_ref, fresh_value_ref = refs[3 + count : 7 + count]
        outs = refs[7 + count : 7 + count + block_count]
        keys_in, values_in, ones, even, odd, largest, result, fresh_in, own_in, sems, fresh_sems = refs[7 + count + block_count :]
        if own_first:
            own_copy = pltpu.make_async_copy(query_refs[0], own_in, fresh_sems.at[2])
            own_copy.start()
            query_refs = (own_in, *query_refs[1:])
        fresh_copies = [
            pltpu.make_async_copy(ref, fresh_in.at[n], fresh_sems.at[n])
            for n, ref in enumerate((fresh_key_ref, fresh_value_ref))
        ]
        for copy in fresh_copies:
            copy.start()
        score_refs = (even, odd)
        filled = bounds_ref[0]
        fresh_start = bounds_ref[1]

        def lane_of(i):
            return pl.multiple_of((blocks_ref[i] // per_key_head) * HD, HD)

        def key_copy(i):
            return pltpu.make_async_copy(
                key_hbm.at[:, pl.ds(lane_of(i), HD)], keys_in.at[i, pl.ds(0, cached)], sems.at[0, i]
            )

        def value_copy(i):
            return pltpu.make_async_copy(
                value_hbm.at[:, pl.ds(lane_of(i), HD)], values_in.at[i, pl.ds(0, cached)], sems.at[1, i]
            )

        key_copy(0).start()
        place = lax.broadcasted_iota(jnp.int32, (padded, HD), 0)
        counted = (place < filled) | ((place >= cached) & (place < cached + fresh))
        ones[...] = jnp.where(counted, 1.0, 0.0).astype(bf16)
        blank = jnp.zeros((128 - fresh, HD), bf16)
        for copy in fresh_copies:
            copy.wait()
        for i in range(block_count):
            lanes = pl.ds(lane_of(i), HD)
            keys_in[i, cached : cached + fresh] = fresh_in[0, :, lanes]
            keys_in[i, cached + fresh :] = blank
            values_in[i, cached : cached + fresh] = fresh_in[1, :, lanes]
            values_in[i, cached + fresh :] = blank
        if own_first:
            own_copy.wait()

        def arrive_keys(i):
            key_copy(i).wait()

        def arrive_values(i):
            value_copy(i).wait()

        def fill_scores(i, slot):
            out = score_refs[slot]
            lanes = pl.ds(pl.multiple_of(blocks_ref[i] * width, HD), width)
            chunks = [ref[:, lanes].astype(f32) * score_scale for ref in query_refs]
            stacked = jnp.concatenate([c[:, h * HD : (h + 1) * HD] for c in chunks for h in range(heads)], 0)
            high = stacked.astype(bf16)
            both = jnp.concatenate([high, (stacked - high.astype(f32)).astype(bf16)], 1)
            running = None
            first = jnp.broadcast_to(keys_in[i, :1], (key_step, HD))
            for start in range(0, cached, key_step):
                part = keys_in[i, start : start + key_step]
                part = jnp.where(ones[start : start + key_step] > 0, part, first)
                scores = scored(both, jnp.concatenate([part, part], 1))
                out[:, start : start + key_step] = scores
                for at in range(0, key_step, HD):
                    piece = scores[:, at : at + HD]
                    running = piece if running is None else jnp.maximum(running, piece)
            part = keys_in[i, cached:]
            scores = scored(both, jnp.concatenate([part, part], 1))
            row = lax.broadcasted_iota(jnp.int32, (rows, HD), 0)
            column = lax.broadcasted_iota(jnp.int32, (rows, HD), 1)
            masked = []
            for c in range(count):
                seen = (column < fresh) & (column + fresh_start <= row + places_ref[c] * rows)
                own = scores[c * heads * rows : (c + 1) * heads * rows]
                masked.append(jnp.where(jnp.tile(seen, (heads, 1)), own, masked_score))
            scores = jnp.concatenate(masked, 0)
            out[:, cached:] = scores
            running = jnp.maximum(running, scores)
            top = jnp.maximum(jnp.max(running, 1, keepdims=True), absent)
            largest[slot] = jnp.broadcast_to(top, (size, HD))

        def weigh(i, slot):
            top = largest[slot]
            probs = jnp.exp2(score_refs[slot][...] - top[:, :1]).astype(bf16)
            both = jnp.concatenate([values_in[i] * ones[...], ones[...]], 1)
            total = jnp.dot(probs, both, preferred_element_type=f32)
            lane = lax.broadcasted_iota(jnp.int32, (rows, HD), 1)
            for c in range(count):
                stats = jnp.zeros((rows, HD), f32)
                for h in range(heads):
                    at = (c * heads + h) * rows
                    piece = total[at : at + rows]
                    norm = piece[:, HD:]
                    some = norm > 0
                    safe = jnp.where(some, norm, 1.0)
                    result[c, :, h * HD : (h + 1) * HD] = (piece[:, :HD] / safe).astype(bf16)
                    level = jnp.where(some, top[at : at + rows] + jnp.log2(safe), absent)
                    for k, part in enumerate(three_parts(level)):
                        stats = jnp.where(lane == h + k * heads, part, stats)
                result[c, :, width:] = stats.astype(bf16)
            for n in range(slot, block_count, 2):

                @pl.when(i == n)
                def _():
                    outs[n][...] = result[...]

        arrive_keys(0)
        for i in range(1, block_count):
            key_copy(i).start()
            value_copy(i - 1).start()
        value_copy(block_count - 1).start()
        fill_scores(0, 0)

        def pair(t, carry):
            arrive_keys(2 * t + 1)
            arrive_values(2 * t)
            fill_scores(2 * t + 1, 1)
            weigh(2 * t, 0)

            @pl.when(t < block_count // 2 - 1)
            def _():
                arrive_keys(2 * t + 2)
                arrive_values(2 * t + 1)
                fill_scores(2 * t + 2, 0)
                weigh(2 * t + 1, 1)

            return carry

        lax.fori_loop(0, block_count // 2, pair, 0)
        arrive_values(block_count - 1)
        weigh(block_count - 1, 1)

    return pl.pallas_call(
        body,
        in_specs=[SM] * 3 + [HBM if own_first and n == 0 else VM for n in range(count)] + [HBM] * 4,
        out_specs=[VM] * block_count,
        out_shape=[jax.ShapeDtypeStruct((count, rows, width + HD), bf16)] * block_count,
        scratch_shapes=[
            pltpu.VMEM((block_count, padded, HD), bf16),
            pltpu.VMEM((block_count, padded, HD), bf16),
            pltpu.VMEM((padded, HD), bf16),
            pltpu.VMEM((size, padded), f32),
            pltpu.VMEM((size, padded), f32),
            pltpu.VMEM((2, size, HD), f32),
            pltpu.VMEM((count, rows, width + HD), bf16),
            pltpu.VMEM((2, fresh, KVH * HD), bf16),
            pltpu.VMEM((rows, QH * HD), bf16),
            pltpu.SemaphoreType.DMA((2, block_count)),
            pltpu.SemaphoreType.DMA((3,)),
        ],
        compiler_params=pltpu.CompilerParams(vmem_limit_bytes=12 * size * padded + (16 << 20)),
        cost_estimate=pl.CostEstimate(
            flops=block_count * size * padded * HD * 2 * 16,
            transcendentals=block_count * size * padded,
            bytes_accessed=4 * cached * KVH * HD,
        ),
    )(
        bounds,
        blocks,
        places,
        *[in_hbm(c) if own_first and n == 0 else c for n, c in enumerate(query_chunks)],
        *[in_hbm(a) for a in (keys, values, fresh_keys, fresh_values)],
    )


def project(pieces, weight, heads):
    arrays = []
    where = []
    for chunk in pieces:
        for array, index in chunk:
            found = [n for n, a in enumerate(arrays) if a is array]
            if not found:
                arrays.append(array)
                found = [len(arrays) - 1]
            where.append((found[0], index))
    chunks = len(pieces)
    sources = len(pieces[0])
    rows = arrays[0].shape[1]
    width = heads * HD
    step = 512

    def body(*refs):
        held = refs[: len(arrays)]
        weight_ref = refs[len(arrays)]
        outs = refs[len(arrays) + 1 : len(arrays) + 1 + chunks]
        attention = refs[-1]

        @pl.when(pl.program_id(0) == 0)
        def _():
            for t in range(chunks):
                spots = where[t * sources : (t + 1) * sources]
                levels = []
                for a, c in spots:
                    stats = held[a][c, :, width:].astype(f32)
                    levels.append(
                        stats + pltpu.roll(stats, HD - heads, axis=1) + pltpu.roll(stats, HD - 2 * heads, axis=1)
                    )
                top = functools.reduce(jnp.maximum, levels)
                weights = [jnp.exp2(level - top) for level in levels]
                total = functools.reduce(jnp.add, weights)
                weights = [weight / total for weight in weights]
                for h in range(heads):
                    mixed = None
                    for (a, c), weight in zip(spots, weights):
                        term = held[a][c, :, h * HD : (h + 1) * HD].astype(f32) * weight[:, h : h + 1]
                        mixed = term if mixed is None else mixed + term
                    attention[t * rows : (t + 1) * rows, h * HD : (h + 1) * HD] = mixed.astype(bf16)

        result = jnp.dot(attention[...], weight_ref[...], preferred_element_type=f32).astype(bf16)
        for t in range(chunks):
            outs[t][...] = result[t * rows : (t + 1) * rows]

    return pl.pallas_call(
        body,
        grid=(D // step,),
        in_specs=[VM] * len(arrays) + [pl.BlockSpec((width, step), lambda n: (0, n))],
        out_specs=[pl.BlockSpec((rows, step), lambda n: (0, n))] * chunks,
        out_shape=[jax.ShapeDtypeStruct((rows, D), bf16)] * chunks,
        scratch_shapes=[pltpu.VMEM((chunks * rows, width), bf16)],
        name="project",
    )(*arrays, in_hbm(weight))


def normalize(residual, shares, gain, gates, experts):
    rows = residual.shape[0]

    def body(residual_ref, *refs):
        share_refs = refs[: len(shares)]
        gain_ref, gates_ref, hidden_ref, message_ref = refs[len(shares) :]
        hidden = share_refs[0][...].astype(f32)
        for ref in share_refs[1:]:
            hidden = hidden + ref[...].astype(f32)
        hidden = residual_ref[...].astype(f32) + hidden
        hidden_ref[...] = hidden
        power = jnp.mean(hidden * hidden, axis=-1, keepdims=True)
        message_ref[:, :D] = (hidden * lax.rsqrt(power + norm_epsilon) * gain_ref[...]).astype(bf16)
        if experts:
            first, second, third = three_parts(gates_ref[...])
            lane = lax.broadcasted_iota(jnp.int32, first.shape, 1)
            parts = jnp.where(lane < experts, first, jnp.where(lane < 2 * experts, second, third))
            message_ref[:, D:] = parts.astype(bf16)

    return pl.pallas_call(
        body,
        in_specs=[VM] * (len(shares) + 3),
        out_specs=[VM] * 2,
        out_shape=[
            jax.ShapeDtypeStruct((rows, D), f32),
            jax.ShapeDtypeStruct((rows, D + (HD if experts else 0)), bf16),
        ],
        name="normalize",
    )(residual, *shares, gain, gates)


def run_expert(expert, messages, gate_up, down, experts):
    rows = messages[0].shape[0]
    count = len(messages)
    half = count // 2 * rows
    step = 256
    steps = FF // step

    def body(expert_ref, *refs):
        message_refs = refs[:count]
        gate_ref, up_ref, down_ref, kept_ref, sent_ref, features, total = refs[count:]
        stage = pl.program_id(0)

        @pl.when(stage == 0)
        def _():
            for c in range(count):
                features[c * rows : (c + 1) * rows] = message_refs[c][:, :D]

        gate = jnp.dot(features[...], gate_ref[...], preferred_element_type=f32)
        up = jnp.dot(features[...], up_ref[...], preferred_element_type=f32)
        inner = (gate / (1.0 + jnp.exp(-gate)) * up).astype(bf16)

        part = jnp.dot(inner, down_ref[...], preferred_element_type=f32)

        @pl.when(stage == 0)
        def _():
            total[...] = part

        @pl.when(stage > 0)
        def _():
            total[...] += part

        @pl.when(stage == steps - 1)
        def _():
            mine = expert_ref[0]
            lane = lax.broadcasted_iota(jnp.int32, (rows, HD), 1)
            chosen = (lane == mine) | (lane == mine + experts) | (lane == mine + 2 * experts)
            for c in range(count):
                parts = message_refs[c][:, D:].astype(f32)
                weight = jnp.sum(jnp.where(chosen, parts, 0.0), 1, keepdims=True)
                out = total[c * rows : (c + 1) * rows].astype(bf16).astype(f32) * weight
                if c < count // 2:
                    kept_ref[c * rows : (c + 1) * rows] = out
                else:
                    at = c * rows - half
                    sent_ref[at : at + rows] = out.astype(bf16)

    return pl.pallas_call(
        body,
        grid=(steps,),
        in_specs=[SM]
        + [VM] * count
        + [
            pl.BlockSpec((D, step), lambda n: (0, n)),
            pl.BlockSpec((D, step), lambda n: (0, n + steps)),
            pl.BlockSpec((step, D), lambda n: (n, 0)),
        ],
        out_specs=[VM] * 2,
        out_shape=[jax.ShapeDtypeStruct((half, D), f32), jax.ShapeDtypeStruct((half, D), bf16)],
        scratch_shapes=[pltpu.VMEM((count * rows, D), bf16), pltpu.VMEM((count * rows, D), f32)],
        compiler_params=pltpu.CompilerParams(vmem_limit_bytes=36 << 20),
        name="run_expert",
    )(expert, *messages, in_hbm(gate_up), in_hbm(gate_up), in_hbm(down))


def mix_all_rows(message, gate_up, down, experts):
    kv_count = lax.axis_size("kv")
    rows = message.shape[0]
    mine = (lax.axis_index("ep") * kv_count + lax.axis_index("kv")).reshape(1).astype(jnp.int32)
    order = sorted(range(kv_count), key=lambda c: -min(c, kv_count - c))
    here = {k: shifted(message, "kv", k) for k in order}
    across = {k: swapped(here[k], "ep", 2) for k in reversed(order)}
    own = [here[k] for k in order] + [across[k] for k in order]
    paired = {m: swapped(own[m], "ep", 1) for m in reversed(range(len(own)))}
    kept, sent = run_expert(mine, own + [paired[m] for m in range(len(own))], gate_up, down, experts)
    pair = kept + swapped(sent, "ep", 1).astype(f32)
    total = None
    for n, k in enumerate(order):
        at = n * rows
        far = at + kv_count * rows
        part = pair[at : at + rows] + swapped(pair[far : far + rows].astype(bf16), "ep", 2).astype(f32)
        if k:
            part = shifted(part.astype(bf16), "kv", -k).astype(f32)
        total = part if total is None else total + part
    return total


def mix_sent_rows(normed, gate_up, down, expert_ids, route_weights, capacity, experts):
    rows = normed.shape[0]
    pair_expert = expert_ids.reshape(-1)
    one_hot = (pair_expert[:, None] == jnp.arange(experts, dtype=jnp.int32)[None, :]).astype(jnp.int32)
    slot_index = jnp.sum((jnp.cumsum(one_hot, axis=0) - 1) * one_hot, axis=1)
    outbound = (
        jnp.zeros((experts, capacity, D), bf16).at[pair_expert, slot_index].set(jnp.repeat(normed, TOPK, axis=0))
    )
    received = lax.all_to_all(outbound, ("ep", "kv"), split_axis=0, concat_axis=0, tiled=True)
    sources, slots, width = received.shape
    mixed = jnp.dot(received.reshape(sources * slots, width), gate_up, preferred_element_type=f32)
    inner = (jax.nn.silu(mixed[:, :FF]) * mixed[:, FF:]).astype(bf16)
    outputs = jnp.dot(inner, down, preferred_element_type=f32).astype(bf16)
    returned = lax.all_to_all(
        outputs.reshape(sources, slots, width), ("ep", "kv"), split_axis=0, concat_axis=0, tiled=True
    )
    picked = returned[pair_expert, slot_index].reshape(rows, TOPK, D)
    return jnp.einsum("rk,rkd->rd", route_weights, picked.astype(f32))


def shards(
    queries,
    new_keys,
    new_values,
    key_cache,
    value_cache,
    lengths,
    residual_in,
    out_weight,
    norm_gain,
    gate_up_weight,
    down_weight,
    expert_ids,
    route_weights,
):
    kv_count = lax.axis_size("kv")
    kv_place = lax.axis_index("kv")
    ep_count = lax.axis_size("ep")
    experts = ep_count * kv_count
    rows = queries.shape[0]
    cached = key_cache.shape[1]
    heads = QH // kv_count
    assert key_cache.shape[0] == 1 and rows * kv_count == BLOCK

    near_first = sorted(range(kv_count), key=lambda c: min(c, kv_count - c))
    chunks = {}
    waiting = queries
    for c in near_first:
        distance = min(c, kv_count - c)
        if distance == 2:
            waiting = lax.optimization_barrier((queries, chunks[1], chunks[kv_count - 1]))[0]
        chunks[c] = shifted(waiting, "kv", c)
    bounds = jnp.stack([jnp.clip(lengths[0] - kv_place * cached, 0, cached), kv_place * rows]).astype(jnp.int32)
    blocks = (kv_place + 1 + jnp.arange(kv_count, dtype=jnp.int32)) % kv_count
    if kv_count == 4:
        calls = GROUPS
    else:
        calls = [near_first[at : at + 2] for at in range(0, kv_count, 2)]
    shares = {}

    def send(outs, call):
        landed = [shifted(outs[k - 1], "kv", k) for k in range(kv_count)]
        for k in range(kv_count):
            for index, c in enumerate(call):
                shares[k, c] = (landed[k], index)
        return landed

    outs = None
    sent = []
    for call in calls:
        places = jnp.stack([(kv_place - c) % kv_count for c in call]).astype(jnp.int32)
        if outs is not None:
            places, outs, sent = lax.optimization_barrier((places, outs, sent))
            for k, landed in enumerate(sent):
                for index, c in enumerate(earlier):
                    shares[k, c] = (landed, index)
            sent = send(outs, before)
            earlier = before
        outs = attend(
            bounds,
            blocks,
            places,
            [chunks[c] for c in call],
            key_cache[0],
            value_cache[0],
            new_keys,
            new_values,
            heads,
            0 in call,
        )
        before = call
    send(outs, before)
    pieces = [[shares[k, (t - k) % kv_count] for k in range(kv_count)] for t in range(kv_count)]
    projected = project(pieces, out_weight, heads)
    landed = [shifted(projected[t], "kv", -t) for t in range(kv_count)]

    capacity = min(rows, max(2, 2 * rows * TOPK // experts))
    everywhere = capacity == rows and ep_count == 4 and kv_count == 4 and 3 * experts <= HD
    named = expert_ids[:, :, None] == jnp.arange(experts, dtype=jnp.int32)[None, None, :]
    gates = jnp.sum(jnp.where(named, route_weights[:, :, None], 0.0), axis=1)
    if everywhere:
        gates = jnp.pad(jnp.tile(gates, (1, 3)), ((0, 0), (0, HD - 3 * experts)))
    hidden_state, message = normalize(
        residual_in, landed, norm_gain[None], gates, experts if everywhere else 0
    )
    if everywhere:
        mixture = mix_all_rows(message, gate_up_weight[0], down_weight[0], experts)
    else:
        mixture = mix_sent_rows(
            message, gate_up_weight[0], down_weight[0], expert_ids, route_weights, capacity, experts
        )
    return (hidden_state + mixture).astype(bf16)


GROUPS = [[0], [1, 3], [2]]


def solution(mesh):
    placed = (
        P(("group", "ep", "kv"), None),
        P(("group", "ep", "kv"), None),
        P(("group", "ep", "kv"), None),
        P(("group", "ep"), "kv", None),
        P(("group", "ep"), "kv", None),
        P(("group", "ep")),
        P(("group", "ep", "kv"), None),
        P("kv", None),
        P(),
        P(("ep", "kv"), None, None),
        P(("ep", "kv"), None, None),
        P(("group", "ep", "kv"), None),
        P(("group", "ep", "kv"), None),
    )
    return jax.shard_map(
        shards,
        mesh=mesh,
        in_specs=placed,
        out_specs=P(("group", "ep", "kv"), None),
        check_vma=False,
    )
```

```python
import functools
import math

import jax
import jax.numpy as jnp
from jax import lax
from jax.experimental import pallas as pl
from jax.experimental.pallas import tpu as pltpu
from jax.sharding import PartitionSpec as P

D = 2048
QH = 32
KVH = 4
HD = 128
FF = 768
TOPK = 8
BLOCK = 128

absent = -1e30
masked_score = -3e38
norm_epsilon = 1e-06
score_scale = math.log2(math.e) * HD**-0.5
key_step = 512
f32 = jnp.float32
bf16 = jnp.bfloat16

HBM = pl.BlockSpec(memory_space=pltpu.HBM)
VM = pl.BlockSpec(memory_space=pltpu.VMEM)
SM = pl.BlockSpec(memory_space=pltpu.SMEM)


def in_hbm(array):
    return pltpu.with_memory_space_constraint(array, pltpu.HBM)


def shifted(array, axis, by):
    size = lax.axis_size(axis)
    if by % size == 0:
        return array
    return lax.ppermute(array, axis, [(i, (i + by) % size) for i in range(size)])


def swapped(array, axis, bit):
    return lax.ppermute(array, axis, [(i, i ^ bit) for i in range(lax.axis_size(axis))])


def scored(left, right):
    return lax.dot_general(left, right, (((1,), (1,)), ((), ())), preferred_element_type=f32)


def three_parts(value):
    first = value.astype(bf16).astype(f32)
    rest = value - first
    second = rest.astype(bf16).astype(f32)
    return first, second, rest - second


def attend(bounds, blocks, places, query_chunks, keys, values, fresh_keys, fresh_values, heads, own_first):
    count = len(query_chunks)
    rows = query_chunks[0].shape[0]
    block_count = QH // heads
    per_key_head = QH // KVH // heads
    cached = keys.shape[0]
    fresh = fresh_keys.shape[0]
    padded = cached + 128
    width = heads * HD
    size = count * heads * rows

    def body(*refs):
        bounds_ref, blocks_ref, places_ref = refs[:3]
        query_refs = refs[3 : 3 + count]
        key_hbm, value_hbm, fresh_key_ref, fresh_value_ref = refs[3 + count : 7 + count]
        outs = refs[7 + count : 7 + count + block_count]
        keys_in, values_in, ones, even, odd, largest, result, fresh_in, own_in, sems, fresh_sems = refs[7 + count + block_count :]
        if own_first:
            own_copy = pltpu.make_async_copy(query_refs[0], own_in, fresh_sems.at[2])
            own_copy.start()
            query_refs = (own_in, *query_refs[1:])
        fresh_copies = [
            pltpu.make_async_copy(ref, fresh_in.at[n], fresh_sems.at[n])
            for n, ref in enumerate((fresh_key_ref, fresh_value_ref))
        ]
        for copy in fresh_copies:
            copy.start()
        score_refs = (even, odd)
        filled = bounds_ref[0]
        fresh_start = bounds_ref[1]

        def lane_of(i):
            return pl.multiple_of((blocks_ref[i] // per_key_head) * HD, HD)

        def key_copy(i):
            return pltpu.make_async_copy(
                key_hbm.at[:, pl.ds(lane_of(i), HD)], keys_in.at[i, pl.ds(0, cached)], sems.at[0, i]
            )

        def value_copy(i):
            return pltpu.make_async_copy(
                value_hbm.at[:, pl.ds(lane_of(i), HD)], values_in.at[i, pl.ds(0, cached)], sems.at[1, i]
            )

        key_copy(0).start()
        place = lax.broadcasted_iota(jnp.int32, (padded, HD), 0)
        counted = (place < filled) | ((place >= cached) & (place < cached + fresh))
        ones[...] = jnp.where(counted, 1.0, 0.0).astype(bf16)
        blank = jnp.zeros((128 - fresh, HD), bf16)
        for copy in fresh_copies:
            copy.wait()
        for i in range(block_count):
            lanes = pl.ds(lane_of(i), HD)
            keys_in[i, cached : cached + fresh] = fresh_in[0, :, lanes]
            keys_in[i, cached + fresh :] = blank
            values_in[i, cached : cached + fresh] = fresh_in[1, :, lanes]
            values_in[i, cached + fresh :] = blank
        if own_first:
            own_copy.wait()

        def arrive_keys(i):
            key_copy(i).wait()

        def arrive_values(i):
            value_copy(i).wait()

        def fill_scores(i, slot):
            out = score_refs[slot]
            lanes = pl.ds(pl.multiple_of(blocks_ref[i] * width, HD), width)
            chunks = [ref[:, lanes].astype(f32) * score_scale for ref in query_refs]
            stacked = jnp.concatenate([c[:, h * HD : (h + 1) * HD] for c in chunks for h in range(heads)], 0)
            high = stacked.astype(bf16)
            both = jnp.concatenate([high, (stacked - high.astype(f32)).astype(bf16)], 1)
            running = None
            first = jnp.broadcast_to(keys_in[i, :1], (key_step, HD))
            for start in range(0, cached, key_step):
                part = keys_in[i, start : start + key_step]
                part = jnp.where(ones[start : start + key_step] > 0, part, first)
                scores = scored(both, jnp.concatenate([part, part], 1))
                out[:, start : start + key_step] = scores
                for at in range(0, key_step, HD):
                    piece = scores[:, at : at + HD]
                    running = piece if running is None else jnp.maximum(running, piece)
            part = keys_in[i, cached:]
            scores = scored(both, jnp.concatenate([part, part], 1))
            row = lax.broadcasted_iota(jnp.int32, (rows, HD), 0)
            column = lax.broadcasted_iota(jnp.int32, (rows, HD), 1)
            masked = []
            for c in range(count):
                seen = (column < fresh) & (column + fresh_start <= row + places_ref[c] * rows)
                own = scores[c * heads * rows : (c + 1) * heads * rows]
                masked.append(jnp.where(jnp.tile(seen, (heads, 1)), own, masked_score))
            scores = jnp.concatenate(masked, 0)
            out[:, cached:] = scores
            running = jnp.maximum(running, scores)
            top = jnp.maximum(jnp.max(running, 1, keepdims=True), absent)
            largest[slot] = jnp.broadcast_to(top, (size, HD))

        def weigh(i, slot):
            top = largest[slot]
            probs = jnp.exp2(score_refs[slot][...] - top[:, :1]).astype(bf16)
            both = jnp.concatenate([values_in[i] * ones[...], ones[...]], 1)
            total = jnp.dot(probs, both, preferred_element_type=f32)
            lane = lax.broadcasted_iota(jnp.int32, (rows, HD), 1)
            for c in range(count):
                stats = jnp.zeros((rows, HD), f32)
                for h in range(heads):
                    at = (c * heads + h) * rows
                    piece = total[at : at + rows]
                    norm = piece[:, HD:]
                    some = norm > 0
                    safe = jnp.where(some, norm, 1.0)
                    result[c, :, h * HD : (h + 1) * HD] = (piece[:, :HD] / safe).astype(bf16)
                    level = jnp.where(some, top[at : at + rows] + jnp.log2(safe), absent)
                    for k, part in enumerate(three_parts(level)):
                        stats = jnp.where(lane == h + k * heads, part, stats)
                result[c, :, width:] = stats.astype(bf16)
            for n in range(slot, block_count, 2):

                @pl.when(i == n)
                def _():
                    outs[n][...] = result[...]

        arrive_keys(0)
        for i in range(1, block_count):
            key_copy(i).start()
            value_copy(i - 1).start()
        value_copy(block_count - 1).start()
        fill_scores(0, 0)

        def pair(t, carry):
            arrive_keys(2 * t + 1)
            arrive_values(2 * t)
            fill_scores(2 * t + 1, 1)
            weigh(2 * t, 0)

            @pl.when(t < block_count // 2 - 1)
            def _():
                arrive_keys(2 * t + 2)
                arrive_values(2 * t + 1)
                fill_scores(2 * t + 2, 0)
                weigh(2 * t + 1, 1)

            return carry

        lax.fori_loop(0, block_count // 2, pair, 0)
        arrive_values(block_count - 1)
        weigh(block_count - 1, 1)

    return pl.pallas_call(
        body,
        in_specs=[SM] * 3 + [HBM if own_first and n == 0 else VM for n in range(count)] + [HBM] * 4,
        out_specs=[VM] * block_count,
        out_shape=[jax.ShapeDtypeStruct((count, rows, width + HD), bf16)] * block_count,
        scratch_shapes=[
            pltpu.VMEM((block_count, padded, HD), bf16),
            pltpu.VMEM((block_count, padded, HD), bf16),
            pltpu.VMEM((padded, HD), bf16),
            pltpu.VMEM((size, padded), f32),
            pltpu.VMEM((size, padded), f32),
            pltpu.VMEM((2, size, HD), f32),
            pltpu.VMEM((count, rows, width + HD), bf16),
            pltpu.VMEM((2, fresh, KVH * HD), bf16),
            pltpu.VMEM((rows, QH * HD), bf16),
            pltpu.SemaphoreType.DMA((2, block_count)),
            pltpu.SemaphoreType.DMA((3,)),
        ],
        compiler_params=pltpu.CompilerParams(vmem_limit_bytes=12 * size * padded + (16 << 20)),
        cost_estimate=pl.CostEstimate(
            flops=block_count * size * padded * HD * 2 * 16,
            transcendentals=block_count * size * padded,
            bytes_accessed=4 * cached * KVH * HD,
        ),
    )(
        bounds,
        blocks,
        places,
        *[in_hbm(c) if own_first and n == 0 else c for n, c in enumerate(query_chunks)],
        *[in_hbm(a) for a in (keys, values, fresh_keys, fresh_values)],
    )


def project(pieces, weight, heads):
    arrays = []
    where = []
    for chunk in pieces:
        for array, index in chunk:
            found = [n for n, a in enumerate(arrays) if a is array]
            if not found:
                arrays.append(array)
                found = [len(arrays) - 1]
            where.append((found[0], index))
    chunks = len(pieces)
    sources = len(pieces[0])
    rows = arrays[0].shape[1]
    width = heads * HD
    step = 512

    def body(*refs):
        held = refs[: len(arrays)]
        weight_ref = refs[len(arrays)]
        outs = refs[len(arrays) + 1 : len(arrays) + 1 + chunks]
        attention = refs[-1]

        @pl.when(pl.program_id(0) == 0)
        def _():
            for t in range(chunks):
                spots = where[t * sources : (t + 1) * sources]
                levels = []
                for a, c in spots:
                    stats = held[a][c, :, width:].astype(f32)
                    levels.append(
                        stats + pltpu.roll(stats, HD - heads, axis=1) + pltpu.roll(stats, HD - 2 * heads, axis=1)
                    )
                top = functools.reduce(jnp.maximum, levels)
                weights = [jnp.exp2(level - top) for level in levels]
                total = functools.reduce(jnp.add, weights)
                weights = [weight / total for weight in weights]
                for h in range(heads):
                    mixed = None
                    for (a, c), weight in zip(spots, weights):
                        term = held[a][c, :, h * HD : (h + 1) * HD].astype(f32) * weight[:, h : h + 1]
                        mixed = term if mixed is None else mixed + term
                    attention[t * rows : (t + 1) * rows, h * HD : (h + 1) * HD] = mixed.astype(bf16)

        result = jnp.dot(attention[...], weight_ref[...], preferred_element_type=f32).astype(bf16)
        for t in range(chunks):
            outs[t][...] = result[t * rows : (t + 1) * rows]

    return pl.pallas_call(
        body,
        grid=(D // step,),
        in_specs=[VM] * len(arrays) + [pl.BlockSpec((width, step), lambda n: (0, n))],
        out_specs=[pl.BlockSpec((rows, step), lambda n: (0, n))] * chunks,
        out_shape=[jax.ShapeDtypeStruct((rows, D), bf16)] * chunks,
        scratch_shapes=[pltpu.VMEM((chunks * rows, width), bf16)],
        name="project",
    )(*arrays, in_hbm(weight))


def normalize(residual, shares, gain, gates, experts):
    rows = residual.shape[0]

    def body(residual_ref, *refs):
        share_refs = refs[: len(shares)]
        gain_ref, gates_ref, hidden_ref, message_ref = refs[len(shares) :]
        hidden = share_refs[0][...].astype(f32)
        for ref in share_refs[1:]:
            hidden = hidden + ref[...].astype(f32)
        hidden = residual_ref[...].astype(f32) + hidden
        hidden_ref[...] = hidden
        power = jnp.mean(hidden * hidden, axis=-1, keepdims=True)
        message_ref[:, :D] = (hidden * lax.rsqrt(power + norm_epsilon) * gain_ref[...]).astype(bf16)
        if experts:
            first, second, third = three_parts(gates_ref[...])
            lane = lax.broadcasted_iota(jnp.int32, first.shape, 1)
            parts = jnp.where(lane < experts, first, jnp.where(lane < 2 * experts, second, third))
            message_ref[:, D:] = parts.astype(bf16)

    return pl.pallas_call(
        body,
        in_specs=[VM] * (len(shares) + 3),
        out_specs=[VM] * 2,
        out_shape=[
            jax.ShapeDtypeStruct((rows, D), f32),
            jax.ShapeDtypeStruct((rows, D + (HD if experts else 0)), bf16),
        ],
        name="normalize",
    )(residual, *shares, gain, gates)


def run_expert(expert, messages, gate_up, down, experts):
    rows = messages[0].shape[0]
    count = len(messages)
    half = count // 2 * rows
    step = 256
    steps = FF // step

    def body(expert_ref, *refs):
        message_refs = refs[:count]
        gate_ref, up_ref, down_hbm, kept_ref, sent_ref, features, inner, down_in, down_sem = refs[count:]
        stage = pl.program_id(0)
        down_copy = pltpu.make_async_copy(down_hbm, down_in, down_sem)

        @pl.when(stage == 0)
        def _():
            down_copy.start()
            for c in range(count):
                features[c * rows : (c + 1) * rows] = message_refs[c][:, :D]

        gate = jnp.dot(features[...], gate_ref[...], preferred_element_type=f32)
        up = jnp.dot(features[...], up_ref[...], preferred_element_type=f32)
        inner[stage] = (gate / (1.0 + jnp.exp(-gate)) * up).astype(bf16)

        @pl.when(stage == steps - 1)
        def _():
            down_copy.wait()
            mine = expert_ref[0]
            lane = lax.broadcasted_iota(jnp.int32, (rows, HD), 1)
            chosen = (lane == mine) | (lane == mine + experts) | (lane == mine + 2 * experts)
            joined = jnp.concatenate([inner[n] for n in range(steps)], 1)
            total = jnp.dot(joined, down_in[...], preferred_element_type=f32)
            for c in range(count):
                parts = message_refs[c][:, D:].astype(f32)
                weight = jnp.sum(jnp.where(chosen, parts, 0.0), 1, keepdims=True)
                out = total[c * rows : (c + 1) * rows].astype(bf16).astype(f32) * weight
                if c < count // 2:
                    kept_ref[c * rows : (c + 1) * rows] = out
                else:
                    at = c * rows - half
                    sent_ref[at : at + rows] = out.astype(bf16)

    return pl.pallas_call(
        body,
        grid=(steps,),
        in_specs=[SM]
        + [VM] * count
        + [
            pl.BlockSpec((D, step), lambda n: (0, n)),
            pl.BlockSpec((D, step), lambda n: (0, n + steps)),
            HBM,
        ],
        out_specs=[VM] * 2,
        out_shape=[jax.ShapeDtypeStruct((half, D), f32), jax.ShapeDtypeStruct((half, D), bf16)],
        scratch_shapes=[
            pltpu.VMEM((count * rows, D), bf16),
            pltpu.VMEM((steps, count * rows, step), bf16),
            pltpu.VMEM((FF, D), bf16),
            pltpu.SemaphoreType.DMA,
        ],
        compiler_params=pltpu.CompilerParams(vmem_limit_bytes=36 << 20),
        name="run_expert",
    )(expert, *messages, in_hbm(gate_up), in_hbm(gate_up), in_hbm(down))


def mix_all_rows(message, gate_up, down, experts):
    kv_count = lax.axis_size("kv")
    rows = message.shape[0]
    mine = (lax.axis_index("ep") * kv_count + lax.axis_index("kv")).reshape(1).astype(jnp.int32)
    order = sorted(range(kv_count), key=lambda c: -min(c, kv_count - c))
    here = {k: shifted(message, "kv", k) for k in order}
    across = {k: swapped(here[k], "ep", 2) for k in reversed(order)}
    own = [here[k] for k in order] + [across[k] for k in order]
    paired = {m: swapped(own[m], "ep", 1) for m in reversed(range(len(own)))}
    kept, sent = run_expert(mine, own + [paired[m] for m in range(len(own))], gate_up, down, experts)
    pair = kept + swapped(sent, "ep", 1).astype(f32)
    total = None
    for n, k in enumerate(order):
        at = n * rows
        far = at + kv_count * rows
        part = pair[at : at + rows] + swapped(pair[far : far + rows].astype(bf16), "ep", 2).astype(f32)
        if k:
            part = shifted(part.astype(bf16), "kv", -k).astype(f32)
        total = part if total is None else total + part
    return total


def mix_sent_rows(normed, gate_up, down, expert_ids, route_weights, capacity, experts):
    rows = normed.shape[0]
    pair_expert = expert_ids.reshape(-1)
    one_hot = (pair_expert[:, None] == jnp.arange(experts, dtype=jnp.int32)[None, :]).astype(jnp.int32)
    slot_index = jnp.sum((jnp.cumsum(one_hot, axis=0) - 1) * one_hot, axis=1)
    outbound = (
        jnp.zeros((experts, capacity, D), bf16).at[pair_expert, slot_index].set(jnp.repeat(normed, TOPK, axis=0))
    )
    received = lax.all_to_all(outbound, ("ep", "kv"), split_axis=0, concat_axis=0, tiled=True)
    sources, slots, width = received.shape
    mixed = jnp.dot(received.reshape(sources * slots, width), gate_up, preferred_element_type=f32)
    inner = (jax.nn.silu(mixed[:, :FF]) * mixed[:, FF:]).astype(bf16)
    outputs = jnp.dot(inner, down, preferred_element_type=f32).astype(bf16)
    returned = lax.all_to_all(
        outputs.reshape(sources, slots, width), ("ep", "kv"), split_axis=0, concat_axis=0, tiled=True
    )
    picked = returned[pair_expert, slot_index].reshape(rows, TOPK, D)
    return jnp.einsum("rk,rkd->rd", route_weights, picked.astype(f32))


def shards(
    queries,
    new_keys,
    new_values,
    key_cache,
    value_cache,
    lengths,
    residual_in,
    out_weight,
    norm_gain,
    gate_up_weight,
    down_weight,
    expert_ids,
    route_weights,
):
    kv_count = lax.axis_size("kv")
    kv_place = lax.axis_index("kv")
    ep_count = lax.axis_size("ep")
    experts = ep_count * kv_count
    rows = queries.shape[0]
    cached = key_cache.shape[1]
    heads = QH // kv_count
    assert key_cache.shape[0] == 1 and rows * kv_count == BLOCK

    near_first = sorted(range(kv_count), key=lambda c: min(c, kv_count - c))
    chunks = {}
    waiting = queries
    for c in near_first:
        distance = min(c, kv_count - c)
        if distance == 2:
            waiting = lax.optimization_barrier((queries, chunks[1], chunks[kv_count - 1]))[0]
        chunks[c] = shifted(waiting, "kv", c)
    bounds = jnp.stack([jnp.clip(lengths[0] - kv_place * cached, 0, cached), kv_place * rows]).astype(jnp.int32)
    blocks = (kv_place + 1 + jnp.arange(kv_count, dtype=jnp.int32)) % kv_count
    if kv_count == 4:
        calls = GROUPS
    else:
        calls = [near_first[at : at + 2] for at in range(0, kv_count, 2)]
    shares = {}

    def send(outs, call):
        landed = [shifted(outs[k - 1], "kv", k) for k in range(kv_count)]
        for k in range(kv_count):
            for index, c in enumerate(call):
                shares[k, c] = (landed[k], index)
        return landed

    outs = None
    sent = []
    for call in calls:
        places = jnp.stack([(kv_place - c) % kv_count for c in call]).astype(jnp.int32)
        if outs is not None:
            places, outs, sent = lax.optimization_barrier((places, outs, sent))
            for k, landed in enumerate(sent):
                for index, c in enumerate(earlier):
                    shares[k, c] = (landed, index)
            sent = send(outs, before)
            earlier = before
        outs = attend(
            bounds,
            blocks,
            places,
            [chunks[c] for c in call],
            key_cache[0],
            value_cache[0],
            new_keys,
            new_values,
            heads,
            0 in call,
        )
        before = call
    send(outs, before)
    pieces = [[shares[k, (t - k) % kv_count] for k in range(kv_count)] for t in range(kv_count)]
    projected = project(pieces, out_weight, heads)
    landed = [shifted(projected[t], "kv", -t) for t in range(kv_count)]

    capacity = min(rows, max(2, 2 * rows * TOPK // experts))
    everywhere = capacity == rows and ep_count == 4 and kv_count == 4 and 3 * experts <= HD
    named = expert_ids[:, :, None] == jnp.arange(experts, dtype=jnp.int32)[None, None, :]
    gates = jnp.sum(jnp.where(named, route_weights[:, :, None], 0.0), axis=1)
    if everywhere:
        gates = jnp.pad(jnp.tile(gates, (1, 3)), ((0, 0), (0, HD - 3 * experts)))
    hidden_state, message = normalize(
        residual_in, landed, norm_gain[None], gates, experts if everywhere else 0
    )
    if everywhere:
        mixture = mix_all_rows(message, gate_up_weight[0], down_weight[0], experts)
    else:
        mixture = mix_sent_rows(
            message, gate_up_weight[0], down_weight[0], expert_ids, route_weights, capacity, experts
        )
    return (hidden_state + mixture).astype(bf16)


GROUPS = [[0], [1, 3], [2]]


def solution(mesh):
    placed = (
        P(("group", "ep", "kv"), None),
        P(("group", "ep", "kv"), None),
        P(("group", "ep", "kv"), None),
        P(("group", "ep"), "kv", None),
        P(("group", "ep"), "kv", None),
        P(("group", "ep")),
        P(("group", "ep", "kv"), None),
        P("kv", None),
        P(),
        P(("ep", "kv"), None, None),
        P(("ep", "kv"), None, None),
        P(("group", "ep", "kv"), None),
        P(("group", "ep", "kv"), None),
    )
    return jax.shard_map(
        shards,
        mesh=mesh,
        in_specs=placed,
        out_specs=P(("group", "ep", "kv"), None),
        check_vma=False,
    )
```

```python
import functools
import math

import jax
import jax.numpy as jnp
from jax import lax
from jax.experimental import pallas as pl
from jax.experimental.pallas import tpu as pltpu
from jax.sharding import PartitionSpec as P

D = 2048
QH = 32
KVH = 4
HD = 128
FF = 768
TOPK = 8
BLOCK = 128

absent = -1e30
masked_score = -3e38
norm_epsilon = 1e-06
score_scale = math.log2(math.e) * HD**-0.5
key_step = 512
f32 = jnp.float32
bf16 = jnp.bfloat16

HBM = pl.BlockSpec(memory_space=pltpu.HBM)
VM = pl.BlockSpec(memory_space=pltpu.VMEM)
SM = pl.BlockSpec(memory_space=pltpu.SMEM)


def in_hbm(array):
    return pltpu.with_memory_space_constraint(array, pltpu.HBM)


def shifted(array, axis, by):
    size = lax.axis_size(axis)
    if by % size == 0:
        return array
    return lax.ppermute(array, axis, [(i, (i + by) % size) for i in range(size)])


def swapped(array, axis, bit):
    return lax.ppermute(array, axis, [(i, i ^ bit) for i in range(lax.axis_size(axis))])


def scored(left, right):
    return lax.dot_general(left, right, (((1,), (1,)), ((), ())), preferred_element_type=f32)


def three_parts(value):
    first = value.astype(bf16).astype(f32)
    rest = value - first
    second = rest.astype(bf16).astype(f32)
    return first, second, rest - second


def attend(bounds, blocks, places, query_chunks, keys, values, fresh_keys, fresh_values, heads, own_first):
    count = len(query_chunks)
    rows = query_chunks[0].shape[0]
    block_count = QH // heads
    per_key_head = QH // KVH // heads
    cached = keys.shape[0]
    fresh = fresh_keys.shape[0]
    padded = cached + 128
    width = heads * HD
    size = count * heads * rows

    def body(*refs):
        bounds_ref, blocks_ref, places_ref = refs[:3]
        query_refs = refs[3 : 3 + count]
        key_hbm, value_hbm, fresh_key_ref, fresh_value_ref = refs[3 + count : 7 + count]
        outs = refs[7 + count : 7 + count + block_count]
        keys_in, values_in, ones, even, odd, largest, result, fresh_in, own_in, sems, fresh_sems = refs[7 + count + block_count :]
        if own_first:
            own_copy = pltpu.make_async_copy(query_refs[0], own_in, fresh_sems.at[2])
            own_copy.start()
            query_refs = (own_in, *query_refs[1:])
        fresh_copies = [
            pltpu.make_async_copy(ref, fresh_in.at[n], fresh_sems.at[n])
            for n, ref in enumerate((fresh_key_ref, fresh_value_ref))
        ]
        for copy in fresh_copies:
            copy.start()
        score_refs = (even, odd)
        filled = bounds_ref[0]
        fresh_start = bounds_ref[1]

        def lane_of(i):
            return pl.multiple_of((blocks_ref[i] // per_key_head) * HD, HD)

        def key_copy(i):
            return pltpu.make_async_copy(
                key_hbm.at[:, pl.ds(lane_of(i), HD)], keys_in.at[i, pl.ds(0, cached)], sems.at[0, i]
            )

        def value_copy(i):
            return pltpu.make_async_copy(
                value_hbm.at[:, pl.ds(lane_of(i), HD)], values_in.at[i, pl.ds(0, cached)], sems.at[1, i]
            )

        key_copy(0).start()
        place = lax.broadcasted_iota(jnp.int32, (padded, HD), 0)
        counted = (place < filled) | ((place >= cached) & (place < cached + fresh))
        ones[...] = jnp.where(counted, 1.0, 0.0).astype(bf16)
        blank = jnp.zeros((128 - fresh, HD), bf16)
        for copy in fresh_copies:
            copy.wait()
        for i in range(block_count):
            lanes = pl.ds(lane_of(i), HD)
            keys_in[i, cached : cached + fresh] = fresh_in[0, :, lanes]
            keys_in[i, cached + fresh :] = blank
            values_in[i, cached : cached + fresh] = fresh_in[1, :, lanes]
            values_in[i, cached + fresh :] = blank
        if own_first:
            own_copy.wait()

        def arrive_keys(i):
            key_copy(i).wait()

        def arrive_values(i):
            value_copy(i).wait()

        def fill_scores(i, slot):
            out = score_refs[slot]
            lanes = pl.ds(pl.multiple_of(blocks_ref[i] * width, HD), width)
            chunks = [ref[:, lanes].astype(f32) * score_scale for ref in query_refs]
            stacked = jnp.concatenate([c[:, h * HD : (h + 1) * HD] for c in chunks for h in range(heads)], 0)
            high = stacked.astype(bf16)
            both = jnp.concatenate([high, (stacked - high.astype(f32)).astype(bf16)], 1)
            running = None
            first = jnp.broadcast_to(keys_in[i, :1], (key_step, HD))
            for start in range(0, cached, key_step):
                part = keys_in[i, start : start + key_step]
                part = jnp.where(ones[start : start + key_step] > 0, part, first)
                scores = scored(both, jnp.concatenate([part, part], 1))
                out[:, start : start + key_step] = scores
                for at in range(0, key_step, HD):
                    piece = scores[:, at : at + HD]
                    running = piece if running is None else jnp.maximum(running, piece)
            part = keys_in[i, cached:]
            scores = scored(both, jnp.concatenate([part, part], 1))
            row = lax.broadcasted_iota(jnp.int32, (rows, HD), 0)
            column = lax.broadcasted_iota(jnp.int32, (rows, HD), 1)
            masked = []
            for c in range(count):
                seen = (column < fresh) & (column + fresh_start <= row + places_ref[c] * rows)
                own = scores[c * heads * rows : (c + 1) * heads * rows]
                masked.append(jnp.where(jnp.tile(seen, (heads, 1)), own, masked_score))
            scores = jnp.concatenate(masked, 0)
            out[:, cached:] = scores
            running = jnp.maximum(running, scores)
            top = jnp.maximum(jnp.max(running, 1, keepdims=True), absent)
            largest[slot] = jnp.broadcast_to(top, (size, HD))

        def weigh(i, slot):
            top = largest[slot]
            probs = jnp.exp2(score_refs[slot][...] - top[:, :1]).astype(bf16)
            both = jnp.concatenate([values_in[i] * ones[...], ones[...]], 1)
            total = jnp.dot(probs, both, preferred_element_type=f32)
            lane = lax.broadcasted_iota(jnp.int32, (rows, HD), 1)
            for c in range(count):
                stats = jnp.zeros((rows, HD), f32)
                for h in range(heads):
                    at = (c * heads + h) * rows
                    piece = total[at : at + rows]
                    norm = piece[:, HD:]
                    some = norm > 0
                    safe = jnp.where(some, norm, 1.0)
                    result[c, :, h * HD : (h + 1) * HD] = (piece[:, :HD] / safe).astype(bf16)
                    level = jnp.where(some, top[at : at + rows] + jnp.log2(safe), absent)
                    for k, part in enumerate(three_parts(level)):
                        stats = jnp.where(lane == h + k * heads, part, stats)
                result[c, :, width:] = stats.astype(bf16)
            for n in range(slot, block_count, 2):

                @pl.when(i == n)
                def _():
                    outs[n][...] = result[...]

        arrive_keys(0)
        for i in range(1, block_count):
            key_copy(i).start()
            value_copy(i - 1).start()
        value_copy(block_count - 1).start()
        fill_scores(0, 0)

        def pair(t, carry):
            arrive_keys(2 * t + 1)
            arrive_values(2 * t)
            fill_scores(2 * t + 1, 1)
            weigh(2 * t, 0)

            @pl.when(t < block_count // 2 - 1)
            def _():
                arrive_keys(2 * t + 2)
                arrive_values(2 * t + 1)
                fill_scores(2 * t + 2, 0)
                weigh(2 * t + 1, 1)

            return carry

        lax.fori_loop(0, block_count // 2, pair, 0)
        arrive_values(block_count - 1)
        weigh(block_count - 1, 1)

    return pl.pallas_call(
        body,
        in_specs=[SM] * 3 + [HBM if own_first and n == 0 else VM for n in range(count)] + [HBM] * 4,
        out_specs=[VM] * block_count,
        out_shape=[jax.ShapeDtypeStruct((count, rows, width + HD), bf16)] * block_count,
        scratch_shapes=[
            pltpu.VMEM((block_count, padded, HD), bf16),
            pltpu.VMEM((block_count, padded, HD), bf16),
            pltpu.VMEM((padded, HD), bf16),
            pltpu.VMEM((size, padded), f32),
            pltpu.VMEM((size, padded), f32),
            pltpu.VMEM((2, size, HD), f32),
            pltpu.VMEM((count, rows, width + HD), bf16),
            pltpu.VMEM((2, fresh, KVH * HD), bf16),
            pltpu.VMEM((rows, QH * HD), bf16),
            pltpu.SemaphoreType.DMA((2, block_count)),
            pltpu.SemaphoreType.DMA((3,)),
        ],
        compiler_params=pltpu.CompilerParams(vmem_limit_bytes=12 * size * padded + (16 << 20)),
        cost_estimate=pl.CostEstimate(
            flops=block_count * size * padded * HD * 2 * 16,
            transcendentals=block_count * size * padded,
            bytes_accessed=4 * cached * KVH * HD,
        ),
    )(
        bounds,
        blocks,
        places,
        *[in_hbm(c) if own_first and n == 0 else c for n, c in enumerate(query_chunks)],
        *[in_hbm(a) for a in (keys, values, fresh_keys, fresh_values)],
    )


def project(pieces, weight, heads):
    arrays = []
    where = []
    for chunk in pieces:
        for array, index in chunk:
            found = [n for n, a in enumerate(arrays) if a is array]
            if not found:
                arrays.append(array)
                found = [len(arrays) - 1]
            where.append((found[0], index))
    chunks = len(pieces)
    sources = len(pieces[0])
    rows = arrays[0].shape[1]
    width = heads * HD
    step = 1024

    def body(*refs):
        held = refs[: len(arrays)]
        weight_ref = refs[len(arrays)]
        outs = refs[len(arrays) + 1 : len(arrays) + 1 + chunks]
        attention = refs[-1]

        @pl.when(pl.program_id(0) == 0)
        def _():
            for t in range(chunks):
                spots = where[t * sources : (t + 1) * sources]
                levels = []
                for a, c in spots:
                    stats = held[a][c, :, width:].astype(f32)
                    levels.append(
                        stats + pltpu.roll(stats, HD - heads, axis=1) + pltpu.roll(stats, HD - 2 * heads, axis=1)
                    )
                top = functools.reduce(jnp.maximum, levels)
                weights = [jnp.exp2(level - top) for level in levels]
                total = functools.reduce(jnp.add, weights)
                weights = [weight / total for weight in weights]
                for h in range(heads):
                    mixed = None
                    for (a, c), weight in zip(spots, weights):
                        term = held[a][c, :, h * HD : (h + 1) * HD].astype(f32) * weight[:, h : h + 1]
                        mixed = term if mixed is None else mixed + term
                    attention[t * rows : (t + 1) * rows, h * HD : (h + 1) * HD] = mixed.astype(bf16)

        result = jnp.dot(attention[...], weight_ref[...], preferred_element_type=f32).astype(bf16)
        for t in range(chunks):
            outs[t][...] = result[t * rows : (t + 1) * rows]

    return pl.pallas_call(
        body,
        grid=(D // step,),
        in_specs=[VM] * len(arrays) + [pl.BlockSpec((width, step), lambda n: (0, n))],
        out_specs=[pl.BlockSpec((rows, step), lambda n: (0, n))] * chunks,
        out_shape=[jax.ShapeDtypeStruct((rows, D), bf16)] * chunks,
        scratch_shapes=[pltpu.VMEM((chunks * rows, width), bf16)],
        compiler_params=pltpu.CompilerParams(vmem_limit_bytes=20 << 20),
        name="project",
    )(*arrays, in_hbm(weight))


def normalize(residual, shares, gain, gates, experts):
    rows = residual.shape[0]

    def body(residual_ref, *refs):
        share_refs = refs[: len(shares)]
        gain_ref, gates_ref, hidden_ref, message_ref = refs[len(shares) :]
        hidden = share_refs[0][...].astype(f32)
        for ref in share_refs[1:]:
            hidden = hidden + ref[...].astype(f32)
        hidden = residual_ref[...].astype(f32) + hidden
        hidden_ref[...] = hidden
        power = jnp.mean(hidden * hidden, axis=-1, keepdims=True)
        message_ref[:, :D] = (hidden * lax.rsqrt(power + norm_epsilon) * gain_ref[...]).astype(bf16)
        if experts:
            first, second, third = three_parts(gates_ref[...])
            lane = lax.broadcasted_iota(jnp.int32, first.shape, 1)
            parts = jnp.where(lane < experts, first, jnp.where(lane < 2 * experts, second, third))
            message_ref[:, D:] = parts.astype(bf16)

    return pl.pallas_call(
        body,
        in_specs=[VM] * (len(shares) + 3),
        out_specs=[VM] * 2,
        out_shape=[
            jax.ShapeDtypeStruct((rows, D), f32),
            jax.ShapeDtypeStruct((rows, D + (HD if experts else 0)), bf16),
        ],
        compiler_params=pltpu.CompilerParams(vmem_limit_bytes=12 << 20),
        name="normalize",
    )(residual, *shares, gain, gates)


def run_expert(expert, messages, gate_up, down, experts):
    rows = messages[0].shape[0]
    count = len(messages)
    half = count // 2 * rows
    step = 256
    steps = FF // step

    def body(expert_ref, *refs):
        message_refs = refs[:count]
        gate_ref, up_ref, down_hbm, kept_ref, sent_ref, features, inner, down_in, down_sem = refs[count:]
        stage = pl.program_id(0)
        down_copy = pltpu.make_async_copy(down_hbm, down_in, down_sem)

        @pl.when(stage == 0)
        def _():
            down_copy.start()
            for c in range(count):
                features[c * rows : (c + 1) * rows] = message_refs[c][:, :D]

        gate = jnp.dot(features[...], gate_ref[...], preferred_element_type=f32)
        up = jnp.dot(features[...], up_ref[...], preferred_element_type=f32)
        inner[stage] = (gate / (1.0 + jnp.exp(-gate)) * up).astype(bf16)

        @pl.when(stage == steps - 1)
        def _():
            down_copy.wait()
            mine = expert_ref[0]
            lane = lax.broadcasted_iota(jnp.int32, (rows, HD), 1)
            chosen = (lane == mine) | (lane == mine + experts) | (lane == mine + 2 * experts)
            joined = jnp.concatenate([inner[n] for n in range(steps)], 1)
            total = jnp.dot(joined, down_in[...], preferred_element_type=f32)
            for c in range(count):
                parts = message_refs[c][:, D:].astype(f32)
                weight = jnp.sum(jnp.where(chosen, parts, 0.0), 1, keepdims=True)
                out = total[c * rows : (c + 1) * rows].astype(bf16).astype(f32) * weight
                if c < count // 2:
                    kept_ref[c * rows : (c + 1) * rows] = out
                else:
                    at = c * rows - half
                    sent_ref[at : at + rows] = out.astype(bf16)

    return pl.pallas_call(
        body,
        grid=(steps,),
        in_specs=[SM]
        + [VM] * count
        + [
            pl.BlockSpec((D, step), lambda n: (0, n)),
            pl.BlockSpec((D, step), lambda n: (0, n + steps)),
            HBM,
        ],
        out_specs=[VM] * 2,
        out_shape=[jax.ShapeDtypeStruct((half, D), f32), jax.ShapeDtypeStruct((half, D), bf16)],
        scratch_shapes=[
            pltpu.VMEM((count * rows, D), bf16),
            pltpu.VMEM((steps, count * rows, step), bf16),
            pltpu.VMEM((FF, D), bf16),
            pltpu.SemaphoreType.DMA,
        ],
        compiler_params=pltpu.CompilerParams(vmem_limit_bytes=36 << 20),
        name="run_expert",
    )(expert, *messages, in_hbm(gate_up), in_hbm(gate_up), in_hbm(down))


def mix_all_rows(message, gate_up, down, experts):
    kv_count = lax.axis_size("kv")
    rows = message.shape[0]
    mine = (lax.axis_index("ep") * kv_count + lax.axis_index("kv")).reshape(1).astype(jnp.int32)
    order = sorted(range(kv_count), key=lambda c: -min(c, kv_count - c))
    here = {k: shifted(message, "kv", k) for k in order}
    across = {k: swapped(here[k], "ep", 2) for k in reversed(order)}
    own = [here[k] for k in order] + [across[k] for k in order]
    paired = {m: swapped(own[m], "ep", 1) for m in reversed(range(len(own)))}
    kept, sent = run_expert(mine, own + [paired[m] for m in range(len(own))], gate_up, down, experts)
    pair = kept + swapped(sent, "ep", 1).astype(f32)
    total = None
    for n, k in enumerate(order):
        at = n * rows
        far = at + kv_count * rows
        part = pair[at : at + rows] + swapped(pair[far : far + rows].astype(bf16), "ep", 2).astype(f32)
        if k:
            part = shifted(part.astype(bf16), "kv", -k).astype(f32)
        total = part if total is None else total + part
    return total


def mix_sent_rows(normed, gate_up, down, expert_ids, route_weights, capacity, experts):
    rows = normed.shape[0]
    pair_expert = expert_ids.reshape(-1)
    one_hot = (pair_expert[:, None] == jnp.arange(experts, dtype=jnp.int32)[None, :]).astype(jnp.int32)
    slot_index = jnp.sum((jnp.cumsum(one_hot, axis=0) - 1) * one_hot, axis=1)
    outbound = (
        jnp.zeros((experts, capacity, D), bf16).at[pair_expert, slot_index].set(jnp.repeat(normed, TOPK, axis=0))
    )
    received = lax.all_to_all(outbound, ("ep", "kv"), split_axis=0, concat_axis=0, tiled=True)
    sources, slots, width = received.shape
    mixed = jnp.dot(received.reshape(sources * slots, width), gate_up, preferred_element_type=f32)
    inner = (jax.nn.silu(mixed[:, :FF]) * mixed[:, FF:]).astype(bf16)
    outputs = jnp.dot(inner, down, preferred_element_type=f32).astype(bf16)
    returned = lax.all_to_all(
        outputs.reshape(sources, slots, width), ("ep", "kv"), split_axis=0, concat_axis=0, tiled=True
    )
    picked = returned[pair_expert, slot_index].reshape(rows, TOPK, D)
    return jnp.einsum("rk,rkd->rd", route_weights, picked.astype(f32))


def shards(
    queries,
    new_keys,
    new_values,
    key_cache,
    value_cache,
    lengths,
    residual_in,
    out_weight,
    norm_gain,
    gate_up_weight,
    down_weight,
    expert_ids,
    route_weights,
):
    kv_count = lax.axis_size("kv")
    kv_place = lax.axis_index("kv")
    ep_count = lax.axis_size("ep")
    experts = ep_count * kv_count
    rows = queries.shape[0]
    cached = key_cache.shape[1]
    heads = QH // kv_count
    assert key_cache.shape[0] == 1 and rows * kv_count == BLOCK

    near_first = sorted(range(kv_count), key=lambda c: min(c, kv_count - c))
    chunks = {}
    waiting = queries
    for c in near_first:
        distance = min(c, kv_count - c)
        if distance == 2:
            waiting = lax.optimization_barrier((queries, chunks[1], chunks[kv_count - 1]))[0]
        chunks[c] = shifted(waiting, "kv", c)
    bounds = jnp.stack([jnp.clip(lengths[0] - kv_place * cached, 0, cached), kv_place * rows]).astype(jnp.int32)
    blocks = (kv_place + 1 + jnp.arange(kv_count, dtype=jnp.int32)) % kv_count
    if kv_count == 4:
        calls = GROUPS
    else:
        calls = [near_first[at : at + 2] for at in range(0, kv_count, 2)]
    shares = {}

    def send(outs, call):
        landed = [shifted(outs[k - 1], "kv", k) for k in range(kv_count)]
        for k in range(kv_count):
            for index, c in enumerate(call):
                shares[k, c] = (landed[k], index)
        return landed

    outs = None
    sent = []
    for call in calls:
        places = jnp.stack([(kv_place - c) % kv_count for c in call]).astype(jnp.int32)
        if outs is not None:
            places, outs, sent = lax.optimization_barrier((places, outs, sent))
            for k, landed in enumerate(sent):
                for index, c in enumerate(earlier):
                    shares[k, c] = (landed, index)
            sent = send(outs, before)
            earlier = before
        outs = attend(
            bounds,
            blocks,
            places,
            [chunks[c] for c in call],
            key_cache[0],
            value_cache[0],
            new_keys,
            new_values,
            heads,
            0 in call,
        )
        before = call
    send(outs, before)
    pieces = [[shares[k, (t - k) % kv_count] for k in range(kv_count)] for t in range(kv_count)]
    projected = project(pieces, out_weight, heads)
    landed = [shifted(projected[t], "kv", -t) for t in range(kv_count)]

    capacity = min(rows, max(2, 2 * rows * TOPK // experts))
    everywhere = capacity == rows and ep_count == 4 and kv_count == 4 and 3 * experts <= HD
    named = expert_ids[:, :, None] == jnp.arange(experts, dtype=jnp.int32)[None, None, :]
    gates = jnp.sum(jnp.where(named, route_weights[:, :, None], 0.0), axis=1)
    if everywhere:
        gates = jnp.pad(jnp.tile(gates, (1, 3)), ((0, 0), (0, HD - 3 * experts)))
    hidden_state, message = normalize(
        residual_in, landed, norm_gain[None], gates, experts if everywhere else 0
    )
    if everywhere:
        mixture = mix_all_rows(message, gate_up_weight[0], down_weight[0], experts)
    else:
        mixture = mix_sent_rows(
            message, gate_up_weight[0], down_weight[0], expert_ids, route_weights, capacity, experts
        )
    return (hidden_state + mixture).astype(bf16)


GROUPS = [[0], [1, 3], [2]]


def solution(mesh):
    placed = (
        P(("group", "ep", "kv"), None),
        P(("group", "ep", "kv"), None),
        P(("group", "ep", "kv"), None),
        P(("group", "ep"), "kv", None),
        P(("group", "ep"), "kv", None),
        P(("group", "ep")),
        P(("group", "ep", "kv"), None),
        P("kv", None),
        P(),
        P(("ep", "kv"), None, None),
        P(("ep", "kv"), None, None),
        P(("group", "ep", "kv"), None),
        P(("group", "ep", "kv"), None),
    )
    return jax.shard_map(
        shards,
        mesh=mesh,
        in_specs=placed,
        out_specs=P(("group", "ep", "kv"), None),
        check_vma=False,
    )
```

```python
import functools
import math

import jax
import jax.numpy as jnp
from jax import lax
from jax.experimental import pallas as pl
from jax.experimental.pallas import tpu as pltpu
from jax.sharding import PartitionSpec as P

D = 2048
QH = 32
KVH = 4
HD = 128
FF = 768
TOPK = 8
BLOCK = 128

absent = -1e30
masked_score = -3e38
norm_epsilon = 1e-06
score_scale = math.log2(math.e) * HD**-0.5
key_step = 512
f32 = jnp.float32
bf16 = jnp.bfloat16

HBM = pl.BlockSpec(memory_space=pltpu.HBM)
VM = pl.BlockSpec(memory_space=pltpu.VMEM)
SM = pl.BlockSpec(memory_space=pltpu.SMEM)


def in_hbm(array):
    return pltpu.with_memory_space_constraint(array, pltpu.HBM)


def shifted(array, axis, by):
    size = lax.axis_size(axis)
    if by % size == 0:
        return array
    return lax.ppermute(array, axis, [(i, (i + by) % size) for i in range(size)])


def swapped(array, axis, bit):
    return lax.ppermute(array, axis, [(i, i ^ bit) for i in range(lax.axis_size(axis))])


def scored(left, right):
    return lax.dot_general(left, right, (((1,), (1,)), ((), ())), preferred_element_type=f32)


def three_parts(value):
    first = value.astype(bf16).astype(f32)
    rest = value - first
    second = rest.astype(bf16).astype(f32)
    return first, second, rest - second


def attend(bounds, blocks, places, query_chunks, keys, values, fresh_keys, fresh_values, heads, own_first):
    count = len(query_chunks)
    rows = query_chunks[0].shape[0]
    block_count = QH // heads
    per_key_head = QH // KVH // heads
    cached = keys.shape[0]
    fresh = fresh_keys.shape[0]
    padded = cached + 128
    width = heads * HD
    size = count * heads * rows

    def body(*refs):
        bounds_ref, blocks_ref, places_ref = refs[:3]
        query_refs = refs[3 : 3 + count]
        key_hbm, value_hbm, fresh_key_ref, fresh_value_ref = refs[3 + count : 7 + count]
        outs = refs[7 + count : 7 + count + block_count]
        keys_in, values_in, ones, even, odd, largest, result, fresh_in, own_in, sems, fresh_sems = refs[7 + count + block_count :]
        if own_first:
            own_copy = pltpu.make_async_copy(query_refs[0], own_in, fresh_sems.at[2])
            own_copy.start()
            query_refs = (own_in, *query_refs[1:])
        fresh_copies = [
            pltpu.make_async_copy(ref, fresh_in.at[n], fresh_sems.at[n])
            for n, ref in enumerate((fresh_key_ref, fresh_value_ref))
        ]
        for copy in fresh_copies:
            copy.start()
        score_refs = (even, odd)
        filled = bounds_ref[0]
        fresh_start = bounds_ref[1]

        def lane_of(i):
            return pl.multiple_of((blocks_ref[i] // per_key_head) * HD, HD)

        def key_copy(i):
            return pltpu.make_async_copy(
                key_hbm.at[:, pl.ds(lane_of(i), HD)], keys_in.at[i, pl.ds(0, cached)], sems.at[0, i]
            )

        def value_copy(i):
            return pltpu.make_async_copy(
                value_hbm.at[:, pl.ds(lane_of(i), HD)], values_in.at[i, pl.ds(0, cached)], sems.at[1, i]
            )

        key_copy(0).start()
        place = lax.broadcasted_iota(jnp.int32, (padded, HD), 0)
        counted = (place < filled) | ((place >= cached) & (place < cached + fresh))
        ones[...] = jnp.where(counted, 1.0, 0.0).astype(bf16)
        blank = jnp.zeros((128 - fresh, HD), bf16)
        for copy in fresh_copies:
            copy.wait()
        for i in range(block_count):
            lanes = pl.ds(lane_of(i), HD)
            keys_in[i, cached : cached + fresh] = fresh_in[0, :, lanes]
            keys_in[i, cached + fresh :] = blank
            values_in[i, cached : cached + fresh] = fresh_in[1, :, lanes]
            values_in[i, cached + fresh :] = blank
        if own_first:
            own_copy.wait()

        def arrive_keys(i):
            key_copy(i).wait()

        def arrive_values(i):
            value_copy(i).wait()

        def fill_scores(i, slot):
            out = score_refs[slot]
            lanes = pl.ds(pl.multiple_of(blocks_ref[i] * width, HD), width)
            chunks = [ref[:, lanes].astype(f32) * score_scale for ref in query_refs]
            stacked = jnp.concatenate([c[:, h * HD : (h + 1) * HD] for c in chunks for h in range(heads)], 0)
            high = stacked.astype(bf16)
            both = jnp.concatenate([high, (stacked - high.astype(f32)).astype(bf16)], 1)
            running = None
            first = jnp.broadcast_to(keys_in[i, :1], (key_step, HD))
            for start in range(0, cached, key_step):
                part = keys_in[i, start : start + key_step]
                part = jnp.where(ones[start : start + key_step] > 0, part, first)
                scores = scored(both, jnp.concatenate([part, part], 1))
                out[:, start : start + key_step] = scores
                for at in range(0, key_step, HD):
                    piece = scores[:, at : at + HD]
                    running = piece if running is None else jnp.maximum(running, piece)
            part = keys_in[i, cached:]
            scores = scored(both, jnp.concatenate([part, part], 1))
            row = lax.broadcasted_iota(jnp.int32, (rows, HD), 0)
            column = lax.broadcasted_iota(jnp.int32, (rows, HD), 1)
            masked = []
            for c in range(count):
                seen = (column < fresh) & (column + fresh_start <= row + places_ref[c] * rows)
                own = scores[c * heads * rows : (c + 1) * heads * rows]
                masked.append(jnp.where(jnp.tile(seen, (heads, 1)), own, masked_score))
            scores = jnp.concatenate(masked, 0)
            out[:, cached:] = scores
            running = jnp.maximum(running, scores)
            top = jnp.maximum(jnp.max(running, 1, keepdims=True), absent)
            largest[slot] = jnp.broadcast_to(top, (size, HD))

        def weigh(i, slot):
            top = largest[slot]
            probs = jnp.exp2(score_refs[slot][...] - top[:, :1]).astype(bf16)
            both = jnp.concatenate([values_in[i] * ones[...], ones[...]], 1)
            total = jnp.dot(probs, both, preferred_element_type=f32)
            lane = lax.broadcasted_iota(jnp.int32, (rows, HD), 1)
            for c in range(count):
                stats = jnp.zeros((rows, HD), f32)
                for h in range(heads):
                    at = (c * heads + h) * rows
                    piece = total[at : at + rows]
                    norm = piece[:, HD:]
                    some = norm > 0
                    safe = jnp.where(some, norm, 1.0)
                    result[c, :, h * HD : (h + 1) * HD] = (piece[:, :HD] / safe).astype(bf16)
                    level = jnp.where(some, top[at : at + rows] + jnp.log2(safe), absent)
                    for k, part in enumerate(three_parts(level)):
                        stats = jnp.where(lane == h + k * heads, part, stats)
                result[c, :, width:] = stats.astype(bf16)
            for n in range(slot, block_count, 2):

                @pl.when(i == n)
                def _():
                    outs[n][...] = result[...]

        arrive_keys(0)
        for i in range(1, block_count):
            key_copy(i).start()
            value_copy(i - 1).start()
        value_copy(block_count - 1).start()
        fill_scores(0, 0)

        def pair(t, carry):
            arrive_keys(2 * t + 1)
            arrive_values(2 * t)
            fill_scores(2 * t + 1, 1)
            weigh(2 * t, 0)

            @pl.when(t < block_count // 2 - 1)
            def _():
                arrive_keys(2 * t + 2)
                arrive_values(2 * t + 1)
                fill_scores(2 * t + 2, 0)
                weigh(2 * t + 1, 1)

            return carry

        lax.fori_loop(0, block_count // 2, pair, 0)
        arrive_values(block_count - 1)
        weigh(block_count - 1, 1)

    return pl.pallas_call(
        body,
        in_specs=[SM] * 3 + [HBM if own_first and n == 0 else VM for n in range(count)] + [HBM] * 4,
        out_specs=[VM] * block_count,
        out_shape=[jax.ShapeDtypeStruct((count, rows, width + HD), bf16)] * block_count,
        scratch_shapes=[
            pltpu.VMEM((block_count, padded, HD), bf16),
            pltpu.VMEM((block_count, padded, HD), bf16),
            pltpu.VMEM((padded, HD), bf16),
            pltpu.VMEM((size, padded), f32),
            pltpu.VMEM((size, padded), f32),
            pltpu.VMEM((2, size, HD), f32),
            pltpu.VMEM((count, rows, width + HD), bf16),
            pltpu.VMEM((2, fresh, KVH * HD), bf16),
            pltpu.VMEM((rows, QH * HD), bf16),
            pltpu.SemaphoreType.DMA((2, block_count)),
            pltpu.SemaphoreType.DMA((3,)),
        ],
        compiler_params=pltpu.CompilerParams(vmem_limit_bytes=10 * size * padded + (13 << 20)),
        cost_estimate=pl.CostEstimate(
            flops=block_count * size * padded * HD * 2 * 16,
            transcendentals=block_count * size * padded,
            bytes_accessed=4 * cached * KVH * HD,
        ),
    )(
        bounds,
        blocks,
        places,
        *[in_hbm(c) if own_first and n == 0 else c for n, c in enumerate(query_chunks)],
        *[in_hbm(a) for a in (keys, values, fresh_keys, fresh_values)],
    )


def project(pieces, weight, heads):
    arrays = []
    where = []
    for chunk in pieces:
        for array, index in chunk:
            found = [n for n, a in enumerate(arrays) if a is array]
            if not found:
                arrays.append(array)
                found = [len(arrays) - 1]
            where.append((found[0], index))
    chunks = len(pieces)
    sources = len(pieces[0])
    rows = arrays[0].shape[1]
    width = heads * HD
    step = 1024

    def body(*refs):
        held = refs[: len(arrays)]
        weight_ref = refs[len(arrays)]
        outs = refs[len(arrays) + 1 : len(arrays) + 1 + chunks]
        attention = refs[-1]

        @pl.when(pl.program_id(0) == 0)
        def _():
            for t in range(chunks):
                spots = where[t * sources : (t + 1) * sources]
                levels = []
                for a, c in spots:
                    stats = held[a][c, :, width:].astype(f32)
                    levels.append(
                        stats + pltpu.roll(stats, HD - heads, axis=1) + pltpu.roll(stats, HD - 2 * heads, axis=1)
                    )
                top = functools.reduce(jnp.maximum, levels)
                weights = [jnp.exp2(level - top) for level in levels]
                total = functools.reduce(jnp.add, weights)
                weights = [weight / total for weight in weights]
                for h in range(heads):
                    mixed = None
                    for (a, c), weight in zip(spots, weights):
                        term = held[a][c, :, h * HD : (h + 1) * HD].astype(f32) * weight[:, h : h + 1]
                        mixed = term if mixed is None else mixed + term
                    attention[t * rows : (t + 1) * rows, h * HD : (h + 1) * HD] = mixed.astype(bf16)

        result = jnp.dot(attention[...], weight_ref[...], preferred_element_type=f32).astype(bf16)
        for t in range(chunks):
            outs[t][...] = result[t * rows : (t + 1) * rows]

    return pl.pallas_call(
        body,
        grid=(D // step,),
        in_specs=[VM] * len(arrays) + [pl.BlockSpec((width, step), lambda n: (0, n))],
        out_specs=[pl.BlockSpec((rows, step), lambda n: (0, n))] * chunks,
        out_shape=[jax.ShapeDtypeStruct((rows, D), bf16)] * chunks,
        scratch_shapes=[pltpu.VMEM((chunks * rows, width), bf16)],
        compiler_params=pltpu.CompilerParams(vmem_limit_bytes=20 << 20),
        name="project",
    )(*arrays, in_hbm(weight))


def normalize(residual, shares, gain, gates, experts):
    rows = residual.shape[0]

    def body(residual_ref, *refs):
        share_refs = refs[: len(shares)]
        gain_ref, gates_ref, hidden_ref, message_ref = refs[len(shares) :]
        hidden = share_refs[0][...].astype(f32)
        for ref in share_refs[1:]:
            hidden = hidden + ref[...].astype(f32)
        hidden = residual_ref[...].astype(f32) + hidden
        hidden_ref[...] = hidden
        power = jnp.mean(hidden * hidden, axis=-1, keepdims=True)
        message_ref[:, :D] = (hidden * lax.rsqrt(power + norm_epsilon) * gain_ref[...]).astype(bf16)
        if experts:
            first, second, third = three_parts(gates_ref[...])
            lane = lax.broadcasted_iota(jnp.int32, first.shape, 1)
            parts = jnp.where(lane < experts, first, jnp.where(lane < 2 * experts, second, third))
            message_ref[:, D:] = parts.astype(bf16)

    return pl.pallas_call(
        body,
        in_specs=[VM] * (len(shares) + 3),
        out_specs=[VM] * 2,
        out_shape=[
            jax.ShapeDtypeStruct((rows, D), f32),
            jax.ShapeDtypeStruct((rows, D + (HD if experts else 0)), bf16),
        ],
        compiler_params=pltpu.CompilerParams(vmem_limit_bytes=12 << 20),
        name="normalize",
    )(residual, *shares, gain, gates)


def run_expert(expert, messages, gate_up, down, experts):
    rows = messages[0].shape[0]
    count = len(messages)
    half = count // 2 * rows
    step = 256
    steps = FF // step

    def body(expert_ref, *refs):
        message_refs = refs[:count]
        gate_ref, up_ref, down_hbm, kept_ref, sent_ref, features, inner, down_in, down_sem = refs[count:]
        stage = pl.program_id(0)
        down_copy = pltpu.make_async_copy(down_hbm, down_in, down_sem)

        @pl.when(stage == 0)
        def _():
            down_copy.start()
            for c in range(count):
                features[c * rows : (c + 1) * rows] = message_refs[c][:, :D]

        gate = jnp.dot(features[...], gate_ref[...], preferred_element_type=f32)
        up = jnp.dot(features[...], up_ref[...], preferred_element_type=f32)
        inner[stage] = (gate / (1.0 + jnp.exp(-gate)) * up).astype(bf16)

        @pl.when(stage == steps - 1)
        def _():
            down_copy.wait()
            mine = expert_ref[0]
            lane = lax.broadcasted_iota(jnp.int32, (rows, HD), 1)
            chosen = (lane == mine) | (lane == mine + experts) | (lane == mine + 2 * experts)
            joined = jnp.concatenate([inner[n] for n in range(steps)], 1)
            total = jnp.dot(joined, down_in[...], preferred_element_type=f32)
            for c in range(count):
                parts = message_refs[c][:, D:].astype(f32)
                weight = jnp.sum(jnp.where(chosen, parts, 0.0), 1, keepdims=True)
                out = total[c * rows : (c + 1) * rows].astype(bf16).astype(f32) * weight
                if c < count // 2:
                    kept_ref[c * rows : (c + 1) * rows] = out
                else:
                    at = c * rows - half
                    sent_ref[at : at + rows] = out.astype(bf16)

    return pl.pallas_call(
        body,
        grid=(steps,),
        in_specs=[SM]
        + [VM] * count
        + [
            pl.BlockSpec((D, step), lambda n: (0, n)),
            pl.BlockSpec((D, step), lambda n: (0, n + steps)),
            HBM,
        ],
        out_specs=[VM] * 2,
        out_shape=[jax.ShapeDtypeStruct((half, D), f32), jax.ShapeDtypeStruct((half, D), bf16)],
        scratch_shapes=[
            pltpu.VMEM((count * rows, D), bf16),
            pltpu.VMEM((steps, count * rows, step), bf16),
            pltpu.VMEM((FF, D), bf16),
            pltpu.SemaphoreType.DMA,
        ],
        compiler_params=pltpu.CompilerParams(vmem_limit_bytes=28 << 20),
        name="run_expert",
    )(expert, *messages, in_hbm(gate_up), in_hbm(gate_up), in_hbm(down))


def mix_all_rows(message, gate_up, down, experts):
    kv_count = lax.axis_size("kv")
    rows = message.shape[0]
    mine = (lax.axis_index("ep") * kv_count + lax.axis_index("kv")).reshape(1).astype(jnp.int32)
    order = sorted(range(kv_count), key=lambda c: -min(c, kv_count - c))
    here = {k: shifted(message, "kv", k) for k in order}
    across = {k: swapped(here[k], "ep", 2) for k in reversed(order)}
    own = [here[k] for k in order] + [across[k] for k in order]
    paired = {m: swapped(own[m], "ep", 1) for m in reversed(range(len(own)))}
    kept, sent = run_expert(mine, own + [paired[m] for m in range(len(own))], gate_up, down, experts)
    pair = kept + swapped(sent, "ep", 1).astype(f32)
    total = None
    for n, k in enumerate(order):
        at = n * rows
        far = at + kv_count * rows
        part = pair[at : at + rows] + swapped(pair[far : far + rows].astype(bf16), "ep", 2).astype(f32)
        if k:
            part = shifted(part.astype(bf16), "kv", -k).astype(f32)
        total = part if total is None else total + part
    return total


def mix_sent_rows(normed, gate_up, down, expert_ids, route_weights, capacity, experts):
    rows = normed.shape[0]
    pair_expert = expert_ids.reshape(-1)
    one_hot = (pair_expert[:, None] == jnp.arange(experts, dtype=jnp.int32)[None, :]).astype(jnp.int32)
    slot_index = jnp.sum((jnp.cumsum(one_hot, axis=0) - 1) * one_hot, axis=1)
    outbound = (
        jnp.zeros((experts, capacity, D), bf16).at[pair_expert, slot_index].set(jnp.repeat(normed, TOPK, axis=0))
    )
    received = lax.all_to_all(outbound, ("ep", "kv"), split_axis=0, concat_axis=0, tiled=True)
    sources, slots, width = received.shape
    mixed = jnp.dot(received.reshape(sources * slots, width), gate_up, preferred_element_type=f32)
    inner = (jax.nn.silu(mixed[:, :FF]) * mixed[:, FF:]).astype(bf16)
    outputs = jnp.dot(inner, down, preferred_element_type=f32).astype(bf16)
    returned = lax.all_to_all(
        outputs.reshape(sources, slots, width), ("ep", "kv"), split_axis=0, concat_axis=0, tiled=True
    )
    picked = returned[pair_expert, slot_index].reshape(rows, TOPK, D)
    return jnp.einsum("rk,rkd->rd", route_weights, picked.astype(f32))


def shards(
    queries,
    new_keys,
    new_values,
    key_cache,
    value_cache,
    lengths,
    residual_in,
    out_weight,
    norm_gain,
    gate_up_weight,
    down_weight,
    expert_ids,
    route_weights,
):
    kv_count = lax.axis_size("kv")
    kv_place = lax.axis_index("kv")
    ep_count = lax.axis_size("ep")
    experts = ep_count * kv_count
    rows = queries.shape[0]
    cached = key_cache.shape[1]
    heads = QH // kv_count
    assert key_cache.shape[0] == 1 and rows * kv_count == BLOCK

    near_first = sorted(range(kv_count), key=lambda c: min(c, kv_count - c))
    chunks = {}
    waiting = queries
    for c in near_first:
        distance = min(c, kv_count - c)
        if distance == 2:
            waiting = lax.optimization_barrier((queries, chunks[1], chunks[kv_count - 1]))[0]
        chunks[c] = shifted(waiting, "kv", c)
    bounds = jnp.stack([jnp.clip(lengths[0] - kv_place * cached, 0, cached), kv_place * rows]).astype(jnp.int32)
    blocks = (kv_place + 1 + jnp.arange(kv_count, dtype=jnp.int32)) % kv_count
    if kv_count == 4:
        calls = GROUPS
    else:
        calls = [near_first[at : at + 2] for at in range(0, kv_count, 2)]
    shares = {}

    def send(outs, call):
        landed = [shifted(outs[k - 1], "kv", k) for k in range(kv_count)]
        for k in range(kv_count):
            for index, c in enumerate(call):
                shares[k, c] = (landed[k], index)
        return landed

    outs = None
    sent = []
    for call in calls:
        places = jnp.stack([(kv_place - c) % kv_count for c in call]).astype(jnp.int32)
        if outs is not None:
            places, outs, sent = lax.optimization_barrier((places, outs, sent))
            for k, landed in enumerate(sent):
                for index, c in enumerate(earlier):
                    shares[k, c] = (landed, index)
            sent = send(outs, before)
            earlier = before
        outs = attend(
            bounds,
            blocks,
            places,
            [chunks[c] for c in call],
            key_cache[0],
            value_cache[0],
            new_keys,
            new_values,
            heads,
            0 in call,
        )
        before = call
    send(outs, before)
    pieces = [[shares[k, (t - k) % kv_count] for k in range(kv_count)] for t in range(kv_count)]
    projected = project(pieces, out_weight, heads)
    landed = [shifted(projected[t], "kv", -t) for t in range(kv_count)]

    capacity = min(rows, max(2, 2 * rows * TOPK // experts))
    everywhere = capacity == rows and ep_count == 4 and kv_count == 4 and 3 * experts <= HD
    named = expert_ids[:, :, None] == jnp.arange(experts, dtype=jnp.int32)[None, None, :]
    gates = jnp.sum(jnp.where(named, route_weights[:, :, None], 0.0), axis=1)
    if everywhere:
        gates = jnp.pad(jnp.tile(gates, (1, 3)), ((0, 0), (0, HD - 3 * experts)))
    hidden_state, message = normalize(
        residual_in, landed, norm_gain[None], gates, experts if everywhere else 0
    )
    if everywhere:
        mixture = mix_all_rows(message, gate_up_weight[0], down_weight[0], experts)
    else:
        mixture = mix_sent_rows(
            message, gate_up_weight[0], down_weight[0], expert_ids, route_weights, capacity, experts
        )
    return (hidden_state + mixture).astype(bf16)


GROUPS = [[0], [1, 3], [2]]


def solution(mesh):
    placed = (
        P(("group", "ep", "kv"), None),
        P(("group", "ep", "kv"), None),
        P(("group", "ep", "kv"), None),
        P(("group", "ep"), "kv", None),
        P(("group", "ep"), "kv", None),
        P(("group", "ep")),
        P(("group", "ep", "kv"), None),
        P("kv", None),
        P(),
        P(("ep", "kv"), None, None),
        P(("ep", "kv"), None, None),
        P(("group", "ep", "kv"), None),
        P(("group", "ep", "kv"), None),
    )
    return jax.shard_map(
        shards,
        mesh=mesh,
        in_specs=placed,
        out_specs=P(("group", "ep", "kv"), None),
        check_vma=False,
    )
```
